512 devices in a mesh: scen: 16 (over z_hi, x, core), col: 32 (over y, z_lo).
Axes of the slice: x: 4, y: 4, z: 16 (z_hi: 2, z_lo: 8; z = z_hi * 8 + z_lo), core: 2. Of those that a mesh axis runs over, the one named last changes fastest.
Arguments:
- coupling: float32 [16, 512, 16384], P('scen', None, 'col'), may hold values from -0.25 to 0.25
- inverse_slabs: float32 [16, 512, 512], P('scen', 'col'), as said below
- barrier_diagonal: float32 [16384], replicated, may hold values from 1 to 16
Outputs:
- panel_factor: float32 [16384, 256], P('col')
The draws below stay inside these ranges and needn't reach their ends.
Inputs may be any that keep to these rules, and one draw needn't show every extreme that they name: `inverse_slabs`: each slab is symmetric positive definite.
All inputs are finite; a program needn't handle non-finite values.
Results may differ from the reference program's by a relative error of at most 0.0001.
Values sent between devices are 32-bit elements; how exact they have to be, the bound alone decides.
No kernel may reach another device: no remote copies, remote signals or barrier semaphores. Data moves between devices by JAX's collectives and lax.ppermute only.
A program may use at most 64 MiB of HBM per device.

```python
import math
import jax
import jax.numpy as jnp
from jax import lax

K = 512
NV = 16384
PANEL = 256
SCEN = 16


def draw_inverse_slabs(key, part):
    base_key = jax.random.fold_in(key, 7)
    key_diag, key_mix = jax.random.split(base_key)
    diag_values = jnp.exp(jax.random.uniform(key_diag, (SCEN, K), jnp.float32, math.log(0.5), math.log(8.0)))
    mixing = jax.random.normal(key_mix, (SCEN, K, K), jnp.float32)

    def one_slab(slab_pair):
        mix_matrix, values = slab_pair
        gram = jnp.dot(mix_matrix, mix_matrix.T, precision=lax.Precision.HIGHEST) / K
        return 0.5 * (gram + gram.T) + jnp.diag(values)
    return lax.map(one_slab, (mixing, diag_values))


def block_levels(key, extent, cuts, least, largest):
    def one(position, blocks):
        heights = jax.random.uniform(jax.random.fold_in(jax.random.fold_in(key, 6), position), (blocks,), jnp.float32, least / len(cuts), largest / len(cuts))
        return jnp.repeat(jnp.exp(heights), extent[position] // blocks).reshape((-1,) + (1,) * (len(extent) - position - 1))

    loudness = one(*cuts[0])
    for cut in cuts[1:]:
        loudness = loudness * one(*cut)
    return loudness


def gaussian(own_key, shape, spread, reach, cuts=(), kind=jnp.bfloat16):
    loudness = block_levels(own_key, shape, cuts, -0.22, 0.18) if cuts else 1.0
    drawn = jax.random.normal(own_key, shape, jnp.float32) * spread * loudness
    return jnp.minimum(jnp.maximum(drawn, -reach), reach).astype(kind)


def setup_inputs(seed: int = 0) -> dict:
    seeds = jax.random.split(jax.random.key(seed), 4)
    return {
        "coupling": gaussian(seeds[0], (SCEN, K, NV), K ** -0.5, 0.25, ((0, 16), (2, 32)), jnp.float32),
        "inverse_slabs": draw_inverse_slabs(jax.random.fold_in(seeds[3], 71), 0),
        "barrier_diagonal": jnp.clip(jnp.exp(jax.random.uniform(seeds[2], (NV,), jnp.float32, math.log(1.0), math.log(16.0))), 1.0, 16.0),
    }


def reference(coupling, inverse_slabs, barrier_diagonal):

    def one_scenario(running, scenario_pair):
        block_matrix, inverse_block = scenario_pair
        solved = jnp.dot(inverse_block.astype(jnp.float32), block_matrix[:, :PANEL].astype(jnp.float32), precision=lax.Precision.HIGHEST, preferred_element_type=jnp.float32)
        update = jnp.dot(block_matrix.T.astype(jnp.float32), solved.astype(jnp.float32), precision=lax.Precision.HIGHEST, preferred_element_type=jnp.float32)
        return (running + update, None)
    partial_value, _ = lax.scan(one_scenario, jnp.zeros((NV, PANEL), jnp.float32), (coupling, inverse_slabs))
    row_ids = jnp.arange(NV, dtype=jnp.int32)[:, None]
    col_ids = jnp.arange(PANEL, dtype=jnp.int32)[None, :]
    schur_rows = partial_value + jnp.where(row_ids == col_ids, barrier_diagonal[:, None], jnp.zeros_like(partial_value))
    top_rows = schur_rows[:PANEL]
    pivot_matrix = 0.5 * (top_rows + top_rows.T)
    factor = jnp.linalg.cholesky(pivot_matrix)
    solved_rows = jax.scipy.linalg.solve_triangular(factor, schur_rows.T, lower=True).T
    return jnp.concatenate([factor, solved_rows[PANEL:]], axis=0)
```

```python
import jax
import jax.numpy as jnp
from jax import lax
from jax.sharding import Mesh, PartitionSpec as P

PANEL = 256
AXES = ("zh", "x", "core", "y", "zl")
HIGHEST = lax.Precision.HIGHEST


def dot(a, b, dims):
    return lax.dot_general(
        a, b, (dims, ((), ())), precision=HIGHEST, preferred_element_type=jnp.float32
    )


def gather(block, axes, count):
    copies = jnp.broadcast_to(block[None], (count,) + block.shape)
    return lax.all_to_all(copies, axes, 0, 0)


def shards(sizes, coupling, inverse_slabs, barrier_diagonal):
    n_zh, n_x, n_core, n_y, n_zl = (sizes[a] for a in AXES)
    n_xc = n_x * n_core
    own = coupling[0]
    depth, width = own.shape
    cols = PANEL // n_y
    y, zl = lax.axis_index("y"), lax.axis_index("zl")

    panel_t = own[:, :PANEL].T.reshape(n_y, cols, depth)
    mine = lax.all_to_all(panel_t, "y", 0, 0)[0]
    mine = jnp.where(zl == 0, mine, 0.0)
    step = n_zl // 2
    while step:
        pairs = [(j, j + step) for j in range(0, n_zl, 2 * step)]
        mine = mine + lax.ppermute(mine, "zl", pairs)
        step //= 2

    inv = gather(inverse_slabs[0], "zl", n_zl).reshape(-1, depth)
    inv = gather(inv, "y", n_y).reshape(depth, depth)

    solved_t = dot(mine, inv, ((1,), (0,)))
    solved_t = gather(solved_t, "y", n_y).reshape(PANEL, depth)

    pivot = dot(mine, solved_t, ((1,), (1,)))
    pivot = lax.all_to_all(pivot.reshape(n_xc, -1, PANEL), ("x", "core"), 0, 0).sum(0)
    pivot = pivot + lax.ppermute(pivot, "zh", [(0, 1), (1, 0)])
    pivot = gather(pivot, ("y", "x", "core"), n_y * n_xc).reshape(PANEL, PANEL)

    rows_t = dot(solved_t, own, ((1,), (0,)))
    rows_t = lax.all_to_all(rows_t.reshape(n_xc, -1, width), ("x", "core"), 0, 0).sum(0)
    rows_t = rows_t + lax.ppermute(rows_t, "zh", [(0, 1), (1, 0)])
    rows_t = gather(rows_t, ("x", "core"), n_xc).reshape(PANEL, width)

    pivot = 0.5 * (pivot + pivot.T) + jnp.diag(barrier_diagonal[:PANEL])
    factor = jnp.linalg.cholesky(pivot)
    solved = jax.scipy.linalg.solve_triangular(factor, rows_t, lower=True).T
    top = jnp.where((y == 0) & (zl == 0), factor, solved[:PANEL])
    return jnp.concatenate([top, solved[PANEL:]], axis=0)


def solution(mesh):
    sizes = {"zh": 2, "x": 4, "core": 2, "y": 4, "zl": 8}
    fine = Mesh(mesh.devices.reshape([sizes[a] for a in AXES]), AXES)

    def run(coupling, inverse_slabs, barrier_diagonal):
        return jax.shard_map(
            lambda *args: shards(sizes, *args),
            mesh=fine,
            in_specs=(
                P(("zh", "x", "core"), None, ("y", "zl")),
                P(("zh", "x", "core"), ("y", "zl"), None),
                P(),
            ),
            out_specs=P(("y", "zl"), None),
            check_vma=False,
        )(coupling, inverse_slabs, barrier_diagonal)

    return run
```

```python
import functools

import jax
import jax.numpy as jnp
from jax import lax
from jax.experimental import pallas as pl
from jax.experimental.pallas import tpu as pltpu
from jax.sharding import Mesh, PartitionSpec as P

PANEL = 256
BLOCK = 64
LANES = 128
AXES = ("zh", "x", "core", "y", "zl")
HIGHEST = lax.Precision.HIGHEST
VMEM = pl.BlockSpec(memory_space=pltpu.VMEM)
PARAMS = pltpu.CompilerParams(vmem_limit_bytes=12 << 20)


def f32(*shape):
    return jax.ShapeDtypeStruct(shape, jnp.float32)


def dot(a, b, da, db):
    return lax.dot_general(
        a, b, (((da,), (db,)), ((), ())), precision=HIGHEST, preferred_element_type=jnp.float32
    )


def call(body, outs, *args, flops=0):
    size = sum(a.size for a in args) * 4
    return pl.pallas_call(
        body,
        compiler_params=PARAMS,
        out_shape=outs,
        in_specs=[VMEM] * len(args),
        out_specs=jax.tree.map(lambda _: VMEM, outs),
        cost_estimate=pl.CostEstimate(flops=flops, bytes_accessed=size, transcendentals=0),
    )(*args)


def lane_of(x, c): return jnp.broadcast_to(x[:, c:c+1], (8, LANES))


def row_of(x, r): return jnp.broadcast_to(x[r:r+1, :], (8, LANES))


def base(tiles, lane0):
    row = lax.broadcasted_iota(jnp.int32, (8, LANES), 0)
    n = len(tiles)
    for s in range(n):
        x = tiles[s]
        cols = [lane_of(x, lane0 + 8*s + j) for j in range(8)]
        rest = [[lane_of(tiles[t], lane0 + 8*s + j) for j in range(8)] for t in range(s+1, n)]
        done = None
        for j in range(8):
            rs = lax.rsqrt(row_of(cols[j], j))
            u = row_of(x, j)
            scaled = u * rs
            g = scaled * rs
            done = scaled if done is None else jnp.where(row >= j, scaled, done)
            x = jnp.where(row == j, g, x - cols[j] * g)
            for l in range(j+1, 8):
                cl = row_of(cols[l], j) * (rs * rs)
                cols[l] = jnp.where(row == j, cl, cols[l] - cols[j] * cl)
        tiles[s] = done
        gs = [row_of(x, j) for j in range(8)]
        for i, t in enumerate(range(s+1, n)):
            acc = tiles[t]
            for j in range(8): acc = acc - rest[i][j] * gs[j]
            tiles[t] = acc
    return tiles


def factor_body(p_ref, diag_ref, m_ref, u_ref):
    a = p_ref[...]
    r = lax.broadcasted_iota(jnp.int32, (PANEL, PANEL), 0)
    c = lax.broadcasted_iota(jnp.int32, (PANEL, PANEL), 1)
    m_ref[...] = 0.5 * (a + a.T) + jnp.where(r == c, diag_ref[...], 0.0)
    lane = lax.broadcasted_iota(jnp.int32, (BLOCK, LANES), 1)
    sub = lax.broadcasted_iota(jnp.int32, (BLOCK, LANES), 0)
    wlane = lax.broadcasted_iota(jnp.int32, (BLOCK, PANEL), 1)
    wsub = lax.broadcasted_iota(jnp.int32, (BLOCK, PANEL), 0)
    for k in range(PANEL // BLOCK):
        odd = k % 2
        seg = m_ref[BLOCK*k:BLOCK*k+BLOCK, LANES*(k//2):LANES*(k//2)+LANES]
        eye = (lane == sub + BLOCK*(1-odd)).astype(jnp.float32)
        own = (lane // BLOCK) == odd
        x = jnp.where(own, seg, eye)
        tiles = base([x[8*t:8*t+8] for t in range(BLOCK//8)], BLOCK*odd)
        x = jnp.concatenate(tiles, axis=0)
        u_ref[BLOCK*k:BLOCK*k+BLOCK, :] = x
        left = jnp.where(own, 0.0, x)
        mrow = m_ref[BLOCK*k:BLOCK*k+BLOCK, :]
        mrow = jnp.where(wlane // BLOCK == k, (wlane == wsub + BLOCK*k).astype(jnp.float32), mrow)
        z = jnp.zeros((BLOCK, PANEL), jnp.float32)
        rhs = jnp.concatenate([mrow, z] if odd else [z, mrow], axis=0)
        nk = lax.dot_general(left, rhs, (((1,),(0,)),((),())), precision=HIGHEST, preferred_element_type=jnp.float32)
        m_ref[BLOCK*k:BLOCK*k+BLOCK, :] = nk
        if k + 1 < PANEL // BLOCK:
            upd = lax.dot_general(nk, nk, (((0,),(0,)),((),())), precision=HIGHEST, preferred_element_type=jnp.float32)
            lo = BLOCK*(k+1)
            below = m_ref[lo:, :]
            wl = lax.broadcasted_iota(jnp.int32, below.shape, 1)
            m_ref[lo:, :] = jnp.where(wl // BLOCK == k, 0.0, below) - upd[lo:, :]


def prepare_body(own_ref, slab_ref, panel_ref, slabs_ref):
    panel_ref[...] = own_ref[0].reshape(panel_ref.shape)
    slabs_ref[...] = jnp.broadcast_to(slab_ref[...], slabs_ref.shape)


def prepare(coupling, slabs, n_y, n_zl):
    _, depth, _ = coupling.shape
    own, slab = (1, depth, PANEL), slabs.shape
    outs = [f32(n_y, depth // n_y, PANEL), f32(n_zl, *slab[1:])]
    return pl.pallas_call(
        prepare_body,
        name="prepare",
        compiler_params=PARAMS,
        grid=(1,),
        out_shape=outs,
        in_specs=[pl.BlockSpec(own, lambda i: (0, 0, 0)), pl.BlockSpec(slab, lambda i: (0, 0, 0))],
        out_specs=[pl.BlockSpec(o.shape, lambda i: (0, 0, 0)) for o in outs],
    )(coupling, slabs)


def copies_body(*refs):
    *ins, out = refs
    total = ins[0][...]
    for ref in ins[1:]:
        total = total + ref[...]
    for i in range(out.shape[0]):
        out[i] = total


def copies(n, *parts):
    return call(copies_body, f32(n, *parts[0].shape), *parts)


def total_body(x_ref, o_ref):
    total = x_ref[0]
    for i in range(1, x_ref.shape[0]):
        total = total + x_ref[i]
    o_ref[...] = total


def total(x):
    return call(total_body, f32(*x.shape[1:]), x)


def solve_body(inv_ref, panel_ref, o_ref):
    rows = dot(inv_ref[...], panel_ref[...], 1, 0)
    for i in range(o_ref.shape[0]):
        o_ref[i] = rows


def product_body(a_ref, b_ref, o_ref):
    o_ref[...] = dot(a_ref[...], b_ref[...], 0, 0).reshape(o_ref.shape)


def finish_body(top_ref, s_ref, m_ref, u_ref, o_ref, left):
    step, per = pl.program_id(0), s_ref.shape[0]
    block = lambda shape, d: lax.broadcasted_iota(jnp.int32, shape, d)

    @pl.when(step == 0)
    def _():
        r, c = block((PANEL, PANEL), 0), block((PANEL, PANEL), 1)
        left[...] = jnp.where(r >= c, m_ref[...], 0.0)

    o_ref[...] = dot(s_ref[...], left[...], 1, 1)

    @pl.when((top_ref[0] == 1) & (step < PANEL // per))
    def _():
        r, c = block((PANEL, LANES), 0), block((PANEL, LANES), 1)
        for half in range(PANEL // LANES):
            lanes = slice(LANES * half, LANES * half + LANES)
            inside = (r // BLOCK) == (c + LANES * half) // BLOCK
            upper = jnp.where(inside, u_ref[...], m_ref[:, lanes])
            upper = jnp.where(r <= c + LANES * half, upper, 0.0).T
            for s in range(LANES // per):
                @pl.when(step == half * (LANES // per) + s)
                def _():
                    o_ref[...] = upper[per * s : per * s + per]


def finish(top, rows, m, u):
    width, per = rows.shape[0], 128
    whole = lambda x: pl.BlockSpec(x.shape, lambda i: (0, 0))
    return pl.pallas_call(
        finish_body,
        name="finish",
        compiler_params=PARAMS,
        grid=(width // per,),
        out_shape=f32(width, PANEL),
        in_specs=[
            pl.BlockSpec(memory_space=pltpu.SMEM),
            pl.BlockSpec((per, PANEL), lambda i: (i, 0)),
            whole(m),
            whole(u),
        ],
        out_specs=pl.BlockSpec((per, PANEL), lambda i: (i, 0)),
        scratch_shapes=[pltpu.VMEM((PANEL, PANEL), jnp.float32)],
        cost_estimate=pl.CostEstimate(
            flops=2 * width * PANEL * PANEL, bytes_accessed=8 * width * PANEL, transcendentals=0
        ),
    )(top, rows, m, u)


def shards(sizes, coupling, inverse_slabs, barrier_diagonal):
    n_zh, n_x, n_core, n_y, n_zl = (sizes[a] for a in AXES)
    n_xc, n_z = n_x * n_core, n_zh * n_zl
    own = coupling[0]
    depth, width = own.shape
    y, zl = lax.axis_index("y"), lax.axis_index("zl")
    swap = functools.partial(lax.all_to_all, split_axis=0, concat_axis=0)

    panel, slabs = prepare(coupling, inverse_slabs, n_y, n_zl)
    inv = swap(slabs, "zl").reshape(-1, depth)

    mine = jnp.where((y == 0) & (zl == 0), panel[0], 0.0)
    parts = []
    for k in range(1, n_y):
        parts.append(lax.ppermute(panel[k], ("y", "zl"), [(0, k * n_zl)]))
    for part in parts:
        mine = mine + part
    step = n_zl // 2
    while step:
        pairs = [(j, j + step) for j in range(0, n_zl, 2 * step)]
        got = lax.ppermute(mine, "zl", pairs)
        if step > 1:
            mine = mine + got
        step //= 2
    panel = swap(copies(n_y, mine, got), "y").reshape(depth, PANEL)

    solved = call(
        solve_body, f32(n_y, depth // n_y, PANEL), inv, panel,
        flops=2 * depth // n_y * depth * PANEL,
    )
    solved = swap(solved, "y").reshape(depth, PANEL)

    pivot = call(
        product_body, f32(n_xc, PANEL // n_xc, PANEL), panel, solved,
        flops=2 * PANEL * depth * PANEL,
    )
    pivot = total(swap(pivot, ("x", "core")))
    half = n_zl // 2
    flip = [(z, (z + (half if z // half % 2 else -half)) % n_z) for z in range(n_z)]
    other = lax.ppermute(pivot, ("zh", "zl"), flip)
    pivot = swap(copies(n_xc, pivot, other), ("x", "core")).reshape(PANEL, PANEL)

    rows = call(
        product_body, f32(n_xc, width // n_xc, PANEL), own, solved,
        flops=2 * width * depth * PANEL,
    )
    rows = total(swap(rows, ("x", "core")))
    other = lax.ppermute(rows, "zh", [(0, 1), (1, 0)])
    rows = swap(copies(n_xc, rows, other), ("x", "core")).reshape(width, PANEL)

    m, u = call(
        factor_body, [f32(PANEL, PANEL), f32(PANEL, LANES)],
        pivot, barrier_diagonal[:PANEL].reshape(1, PANEL),
        flops=6 * 10**9,
    )
    top = ((y == 0) & (zl == 0)).astype(jnp.int32).reshape(1)
    return finish(top, rows, m, u)


def solution(mesh):
    sizes = {"zh": 2, "x": 4, "core": 2, "y": 4, "zl": 8}
    fine = Mesh(mesh.devices.reshape([sizes[a] for a in AXES]), AXES)
    return jax.shard_map(
        functools.partial(shards, sizes),
        mesh=fine,
        in_specs=(
            P(("zh", "x", "core"), None, ("y", "zl")),
            P(("zh", "x", "core"), ("y", "zl"), None),
            P(),
        ),
        out_specs=P(("y", "zl"), None),
        check_vma=False,
    )
```

```python
import functools

import jax
import jax.numpy as jnp
from jax import lax
from jax.experimental import pallas as pl
from jax.experimental.pallas import tpu as pltpu
from jax.sharding import Mesh, PartitionSpec as P

PANEL = 256
BLOCK = 64
LANES = 128
AXES = ("zh", "x", "core", "y", "zl")
HIGHEST = lax.Precision.HIGHEST
VMEM = pl.BlockSpec(memory_space=pltpu.VMEM)
PARAMS = pltpu.CompilerParams(vmem_limit_bytes=12 << 20)


def f32(*shape):
    return jax.ShapeDtypeStruct(shape, jnp.float32)


def dot(a, b, da, db):
    return lax.dot_general(
        a, b, (((da,), (db,)), ((), ())), precision=HIGHEST, preferred_element_type=jnp.float32
    )


def call(body, outs, *args, flops=0):
    size = sum(a.size for a in args) * 4
    return pl.pallas_call(
        body,
        compiler_params=PARAMS,
        out_shape=outs,
        in_specs=[VMEM] * len(args),
        out_specs=jax.tree.map(lambda _: VMEM, outs),
        cost_estimate=pl.CostEstimate(flops=flops, bytes_accessed=size, transcendentals=0),
    )(*args)


def lane_of(x, c): return jnp.broadcast_to(x[:, c:c+1], (8, LANES))


def row_of(x, r): return jnp.broadcast_to(x[r:r+1, :], (8, LANES))


def base(tiles, lane0):
    row = lax.broadcasted_iota(jnp.int32, (8, LANES), 0)
    n = len(tiles)
    for s in range(n):
        x = tiles[s]
        cols = [lane_of(x, lane0 + 8*s + j) for j in range(8)]
        rest = [[lane_of(tiles[t], lane0 + 8*s + j) for j in range(8)] for t in range(s+1, n)]
        done = None
        for j in range(8):
            rs = lax.rsqrt(row_of(cols[j], j))
            u = row_of(x, j)
            scaled = u * rs
            g = scaled * rs
            done = scaled if done is None else jnp.where(row >= j, scaled, done)
            x = jnp.where(row == j, g, x - cols[j] * g)
            for l in range(j+1, 8):
                cl = row_of(cols[l], j) * (rs * rs)
                cols[l] = jnp.where(row == j, cl, cols[l] - cols[j] * cl)
        tiles[s] = done
        gs = [row_of(x, j) for j in range(8)]
        for i, t in enumerate(range(s+1, n)):
            acc = tiles[t]
            for j in range(8): acc = acc - rest[i][j] * gs[j]
            tiles[t] = acc
    return tiles


def factor_body(p_ref, diag_ref, m_ref, u_ref):
    a = p_ref[...]
    r = lax.broadcasted_iota(jnp.int32, (PANEL, PANEL), 0)
    c = lax.broadcasted_iota(jnp.int32, (PANEL, PANEL), 1)
    m_ref[...] = 0.5 * (a + a.T) + jnp.where(r == c, diag_ref[...], 0.0)
    lane = lax.broadcasted_iota(jnp.int32, (BLOCK, LANES), 1)
    sub = lax.broadcasted_iota(jnp.int32, (BLOCK, LANES), 0)
    wlane = lax.broadcasted_iota(jnp.int32, (BLOCK, PANEL), 1)
    wsub = lax.broadcasted_iota(jnp.int32, (BLOCK, PANEL), 0)
    for k in range(PANEL // BLOCK):
        odd = k % 2
        seg = m_ref[BLOCK*k:BLOCK*k+BLOCK, LANES*(k//2):LANES*(k//2)+LANES]
        eye = (lane == sub + BLOCK*(1-odd)).astype(jnp.float32)
        own = (lane // BLOCK) == odd
        x = jnp.where(own, seg, eye)
        tiles = base([x[8*t:8*t+8] for t in range(BLOCK//8)], BLOCK*odd)
        x = jnp.concatenate(tiles, axis=0)
        u_ref[BLOCK*k:BLOCK*k+BLOCK, :] = x
        left = jnp.where(own, 0.0, x)
        mrow = m_ref[BLOCK*k:BLOCK*k+BLOCK, :]
        mrow = jnp.where(wlane // BLOCK == k, (wlane == wsub + BLOCK*k).astype(jnp.float32), mrow)
        z = jnp.zeros((BLOCK, PANEL), jnp.float32)
        rhs = jnp.concatenate([mrow, z] if odd else [z, mrow], axis=0)
        nk = lax.dot_general(left, rhs, (((1,),(0,)),((),())), precision=HIGHEST, preferred_element_type=jnp.float32)
        m_ref[BLOCK*k:BLOCK*k+BLOCK, :] = nk
        if k + 1 < PANEL // BLOCK:
            upd = lax.dot_general(nk, nk, (((0,),(0,)),((),())), precision=HIGHEST, preferred_element_type=jnp.float32)
            lo = BLOCK*(k+1)
            below = m_ref[lo:, :]
            wl = lax.broadcasted_iota(jnp.int32, below.shape, 1)
            m_ref[lo:, :] = jnp.where(wl // BLOCK == k, 0.0, below) - upd[lo:, :]


def copies_body(*refs):
    *ins, out = refs
    total = ins[0][...]
    for ref in ins[1:]:
        total = total + ref[...]
    for i in range(out.shape[0]):
        out[i] = total


def copies(n, *parts):
    return call(copies_body, f32(n, *parts[0].shape), *parts)


def total_body(x_ref, *outs):
    at = 0
    for out in outs:
        rows = slice(at, at + out.shape[0])
        total = x_ref[0, rows]
        for i in range(1, x_ref.shape[0]):
            total = total + x_ref[i, rows]
        out[...] = total
        at += out.shape[0]


def solve_body(inv_ref, panel_ref, o_ref):
    rows = dot(inv_ref[...], panel_ref[...], 1, 0)
    for i in range(o_ref.shape[0]):
        o_ref[i] = rows


def halves(x):
    high = x.astype(jnp.bfloat16)
    return high, (x - high.astype(jnp.float32)).astype(jnp.bfloat16)


def dot_halves(a, b, da, db):
    one = lambda p, q: lax.dot_general(
        p, q, (((da,), (db,)), ((), ())), preferred_element_type=jnp.float32
    )
    return one(a[0], b[0]) + (one(a[0], b[1]) + one(a[1], b[0]))


def turn_body(own_ref, panel_ref, high_ref, low_ref):
    at = 0
    for x in (own_ref[0], panel_ref[...]):
        rows = slice(at, at + x.shape[1])
        high_ref[rows], low_ref[rows] = halves(x.T)
        at += x.shape[1]


def terms_body(high_ref, low_ref, solved_ref, o_ref):
    width = high_ref.shape[0] - PANEL
    s = halves(solved_ref[...])
    n = o_ref.shape[0]
    for at, rows, out in ((0, width, 0), (width, PANEL, width // n)):
        part = slice(at, at + rows)
        x = dot_halves((high_ref[part], low_ref[part]), s, 1, 0)
        o_ref[:, out : out + rows // n] = x.reshape(n, rows // n, PANEL)


def finish_body(top_ref, s_ref, m_ref, u_ref, o_ref, left):
    step, per = pl.program_id(0), s_ref.shape[0]
    block = lambda shape, d: lax.broadcasted_iota(jnp.int32, shape, d)

    @pl.when(step == 0)
    def _():
        r, c = block((PANEL, PANEL), 0), block((PANEL, PANEL), 1)
        left[0], left[1] = halves(jnp.where(r >= c, m_ref[...], 0.0))

    o_ref[...] = dot_halves(halves(s_ref[...]), (left[0], left[1]), 1, 1)

    @pl.when((top_ref[0] == 1) & (step < PANEL // per))
    def _():
        r, c = block((PANEL, LANES), 0), block((PANEL, LANES), 1)
        for half in range(PANEL // LANES):
            lanes = slice(LANES * half, LANES * half + LANES)
            inside = (r // BLOCK) == (c + LANES * half) // BLOCK
            upper = jnp.where(inside, u_ref[...], m_ref[:, lanes])
            upper = jnp.where(r <= c + LANES * half, upper, 0.0).T
            for s in range(LANES // per):
                @pl.when(step == half * (LANES // per) + s)
                def _():
                    o_ref[...] = upper[per * s : per * s + per]


def finish(top, rows, m, u):
    width, per = rows.shape[0], 128
    whole = lambda x: pl.BlockSpec(x.shape, lambda i: (0, 0))
    return pl.pallas_call(
        finish_body,
        name="finish",
        compiler_params=PARAMS,
        grid=(width // per,),
        out_shape=f32(width, PANEL),
        in_specs=[
            pl.BlockSpec(memory_space=pltpu.SMEM),
            pl.BlockSpec((per, PANEL), lambda i: (i, 0)),
            whole(m),
            whole(u),
        ],
        out_specs=pl.BlockSpec((per, PANEL), lambda i: (i, 0)),
        scratch_shapes=[pltpu.VMEM((2, PANEL, PANEL), jnp.bfloat16)],
        cost_estimate=pl.CostEstimate(
            flops=2 * width * PANEL * PANEL, bytes_accessed=8 * width * PANEL, transcendentals=0
        ),
    )(top, rows, m, u)


def shards(sizes, coupling, inverse_slabs, barrier_diagonal):
    n_zh, n_x, n_core, n_y, n_zl = (sizes[a] for a in AXES)
    n_xc, n_z = n_x * n_core, n_zh * n_zl
    own = coupling[0]
    depth, width = own.shape
    y, zl = lax.axis_index("y"), lax.axis_index("zl")
    swap = functools.partial(lax.all_to_all, split_axis=0, concat_axis=0)

    per = depth // n_y
    cut = lambda k: own[per * k : per * k + per, :PANEL]
    parts = []
    for k in range(1, n_y):
        parts.append(lax.ppermute(cut(k), ("y", "zl"), [(0, k * n_zl)]))
    inv = swap(copies(n_zl, inverse_slabs[0]), "zl").reshape(-1, depth)
    mine = jnp.where((y == 0) & (zl == 0), cut(0), 0.0)
    for part in parts:
        mine = mine + part
    step = n_zl // 2
    while step:
        pairs = [(j, j + step) for j in range(0, n_zl, 2 * step)]
        got = lax.ppermute(mine, "zl", pairs)
        if step > 1:
            mine = mine + got
        step //= 2
    panel = swap(copies(n_y, mine, got), "y").reshape(depth, PANEL)

    solved = call(
        solve_body, f32(n_y, depth // n_y, PANEL), inv, panel,
        flops=2 * depth // n_y * depth * PANEL,
    )
    solved = swap(solved, "y").reshape(depth, PANEL)

    high, low = call(
        turn_body, [jax.ShapeDtypeStruct((width + PANEL, depth), jnp.bfloat16)] * 2,
        coupling, panel, flops=10**9,
    )
    n_row, n_piv = width // n_xc, PANEL // n_xc
    terms = call(
        terms_body, f32(n_xc, n_row + n_piv, PANEL), high, low, solved,
        flops=6 * (width + PANEL) * depth * PANEL,
    )
    terms = swap(terms, ("x", "core"))
    rows, pivot = call(total_body, [f32(n_row, PANEL), f32(n_piv, PANEL)], terms)

    half = n_zl // 2
    flip = [(z, (z + (half if z // half % 2 else -half)) % n_z) for z in range(n_z)]
    other = lax.ppermute(pivot, ("zh", "zl"), flip)
    pivot = swap(copies(n_xc, pivot, other), ("x", "core")).reshape(PANEL, PANEL)
    other = lax.ppermute(rows, "zh", [(0, 1), (1, 0)])
    rows = swap(copies(n_xc, rows, other), ("x", "core")).reshape(width, PANEL)

    m, u = call(
        factor_body, [f32(PANEL, PANEL), f32(PANEL, LANES)],
        pivot, barrier_diagonal[:PANEL].reshape(1, PANEL),
        flops=6 * 10**9,
    )
    top = ((y == 0) & (zl == 0)).astype(jnp.int32).reshape(1)
    return finish(top, rows, m, u)


def solution(mesh):
    sizes = {"zh": 2, "x": 4, "core": 2, "y": 4, "zl": 8}
    fine = Mesh(mesh.devices.reshape([sizes[a] for a in AXES]), AXES)
    return jax.shard_map(
        functools.partial(shards, sizes),
        mesh=fine,
        in_specs=(
            P(("zh", "x", "core"), None, ("y", "zl")),
            P(("zh", "x", "core"), ("y", "zl"), None),
            P(),
        ),
        out_specs=P(("y", "zl"), None),
        check_vma=False,
    )
```

```python
import functools

import jax
import jax.numpy as jnp
from jax import lax
from jax.experimental import pallas as pl
from jax.experimental.pallas import tpu as pltpu
from jax.sharding import Mesh, PartitionSpec as P

PANEL = 256
BLOCK = 64
LANES = 128
AXES = ("zh", "x", "core", "y", "zl")
HIGHEST = lax.Precision.HIGHEST
VMEM = pl.BlockSpec(memory_space=pltpu.VMEM)
PARAMS = pltpu.CompilerParams(vmem_limit_bytes=12 << 20)


def f32(*shape):
    return jax.ShapeDtypeStruct(shape, jnp.float32)


def bf16(*shape):
    return jax.ShapeDtypeStruct(shape, jnp.bfloat16)


def call(body, outs, *args, flops=0):
    size = sum(a.size for a in args) * 4
    return pl.pallas_call(
        body,
        compiler_params=PARAMS,
        out_shape=outs,
        in_specs=[VMEM] * len(args),
        out_specs=jax.tree.map(lambda _: VMEM, outs),
        cost_estimate=pl.CostEstimate(flops=flops, bytes_accessed=size, transcendentals=0),
    )(*args)


def lane_of(x, c): return jnp.broadcast_to(x[:, c:c+1], (8, LANES))


def row_of(x, r): return jnp.broadcast_to(x[r:r+1, :], (8, LANES))


def base(tiles, lane0):
    row = lax.broadcasted_iota(jnp.int32, (8, LANES), 0)
    n = len(tiles)
    for s in range(n):
        x = tiles[s]
        cols = [lane_of(x, lane0 + 8*s + j) for j in range(8)]
        rest = [[lane_of(tiles[t], lane0 + 8*s + j) for j in range(8)] for t in range(s+1, n)]
        done = None
        for j in range(8):
            rs = lax.rsqrt(row_of(cols[j], j))
            u = row_of(x, j)
            scaled = u * rs
            g = scaled * rs
            done = scaled if done is None else jnp.where(row >= j, scaled, done)
            x = jnp.where(row == j, g, x - cols[j] * g)
            for l in range(j+1, 8):
                cl = row_of(cols[l], j) * (rs * rs)
                cols[l] = jnp.where(row == j, cl, cols[l] - cols[j] * cl)
        tiles[s] = done
        gs = [row_of(x, j) for j in range(8)]
        for i, t in enumerate(range(s+1, n)):
            acc = tiles[t]
            for j in range(8): acc = acc - rest[i][j] * gs[j]
            tiles[t] = acc
    return tiles


def factor_body(p_ref, diag_ref, m_ref, u_ref):
    half = PANEL // 2
    r = lax.broadcasted_iota(jnp.int32, (half, PANEL), 0)
    c = lax.broadcasted_iota(jnp.int32, (half, PANEL), 1)
    diag = diag_ref[...]
    m_ref[:half] = p_ref[:half] + jnp.where(r == c, diag, 0.0)
    last = p_ref[half:]
    last = jnp.concatenate([last[:, :half], last[:, half:]], axis=0)
    last = jnp.concatenate([jnp.zeros_like(last), last], axis=1)
    m_ref[half:] = last + jnp.where(r + half == c, diag, 0.0)
    lane = lax.broadcasted_iota(jnp.int32, (BLOCK, LANES), 1)
    sub = lax.broadcasted_iota(jnp.int32, (BLOCK, LANES), 0)
    wlane = lax.broadcasted_iota(jnp.int32, (BLOCK, PANEL), 1)
    wsub = lax.broadcasted_iota(jnp.int32, (BLOCK, PANEL), 0)
    for k in range(PANEL // BLOCK):
        odd = k % 2
        seg = m_ref[BLOCK*k:BLOCK*k+BLOCK, LANES*(k//2):LANES*(k//2)+LANES]
        eye = (lane == sub + BLOCK*(1-odd)).astype(jnp.float32)
        own = (lane // BLOCK) == odd
        x = jnp.where(own, seg, eye)
        tiles = base([x[8*t:8*t+8] for t in range(BLOCK//8)], BLOCK*odd)
        x = jnp.concatenate(tiles, axis=0)
        u_ref[BLOCK*k:BLOCK*k+BLOCK, :] = x
        left = jnp.where(own, 0.0, x)
        mrow = m_ref[BLOCK*k:BLOCK*k+BLOCK, :]
        mrow = jnp.where(wlane // BLOCK == k, (wlane == wsub + BLOCK*k).astype(jnp.float32), mrow)
        z = jnp.zeros((BLOCK, PANEL), jnp.float32)
        rhs = jnp.concatenate([mrow, z] if odd else [z, mrow], axis=0)
        nk = lax.dot_general(left, rhs, (((1,),(0,)),((),())), precision=HIGHEST, preferred_element_type=jnp.float32)
        m_ref[BLOCK*k:BLOCK*k+BLOCK, :] = nk
        if k + 1 < PANEL // BLOCK:
            upd = lax.dot_general(nk, nk, (((0,),(0,)),((),())), precision=HIGHEST, preferred_element_type=jnp.float32)
            lo = BLOCK*(k+1)
            below = m_ref[lo:, :]
            wl = lax.broadcasted_iota(jnp.int32, below.shape, 1)
            m_ref[lo:, :] = jnp.where(wl // BLOCK == k, 0.0, below) - upd[lo:, :]


def copies_body(*refs):
    *ins, out = refs
    total = ins[0][...]
    for ref in ins[1:]:
        total = total + ref[...]
    for i in range(out.shape[0]):
        out[i] = total


def sum_body(*refs):
    *ins, out = refs
    total = ins[0][...]
    for ref in ins[1:]:
        total = total + ref[...]
    out[...] = total


def copies(n, *parts):
    return call(copies_body, f32(n, *parts[0].shape), *parts)


def total_body(x_ref, *outs):
    at = 0
    for out in outs:
        rows = slice(at, at + out.shape[0])
        total = x_ref[0, rows]
        for i in range(1, x_ref.shape[0]):
            total = total + x_ref[i, rows]
        out[...] = total
        at += out.shape[0]


def halves(x):
    high = x.astype(jnp.bfloat16)
    return high, (x - high.astype(jnp.float32)).astype(jnp.bfloat16)


def dot_halves(a, b, da, db):
    one = lambda p, q: lax.dot_general(
        p, q, (((da,), (db,)), ((), ())), preferred_element_type=jnp.float32
    )
    return one(a[0], b[0]) + (one(a[0], b[1]) + one(a[1], b[0]))


def turn_body(own_ref, turned_ref):
    turned_ref[0], turned_ref[1] = halves(own_ref[0].T)


def terms_body(turned_ref, inv_ref, panel_ref, o_ref, turned, sem):
    fetch = pltpu.make_async_copy(turned_ref, turned, sem)
    fetch.start()
    panel = panel_ref[...]
    n, half = o_ref.shape[0], PANEL // 2
    s = halves(dot_halves(halves(inv_ref[...]), halves(panel), 1, 0))
    x = dot_halves(halves(panel.T), s, 1, 0)
    last = jnp.concatenate(
        [x[half : half + half // 2, half:], x[half + half // 2 :, half:]], axis=1
    )
    x = jnp.concatenate([x[:half], last], axis=0)
    rows = turned.shape[1] // n
    o_ref[:, rows:] = x.reshape(n, x.shape[0] // n, PANEL)
    fetch.wait()
    x = dot_halves((turned[0], turned[1]), s, 1, 0)
    o_ref[:, :rows] = x.reshape(n, rows, PANEL)


def multiply(turned, inv, panel, n):
    _, width, depth = turned.shape
    return pl.pallas_call(
        terms_body,
        name="terms",
        out_shape=f32(n, (width + 3 * PANEL // 4) // n, PANEL),
        compiler_params=PARAMS,
        in_specs=[pl.BlockSpec(memory_space=pltpu.HBM), VMEM, VMEM],
        out_specs=VMEM,
        scratch_shapes=[pltpu.VMEM(turned.shape, turned.dtype), pltpu.SemaphoreType.DMA],
        cost_estimate=pl.CostEstimate(
            flops=6 * (width + PANEL + depth) * depth * PANEL,
            bytes_accessed=4 * depth * (width + depth),
            transcendentals=0,
        ),
    )(pltpu.with_memory_space_constraint(turned, pltpu.HBM), inv, panel)


def finish_body(top_ref, s_ref, m_ref, u_ref, o_ref, left):
    step, per = pl.program_id(0), s_ref.shape[0]
    block = lambda shape, d: lax.broadcasted_iota(jnp.int32, shape, d)

    @pl.when(step == 0)
    def _():
        r, c = block((PANEL, PANEL), 0), block((PANEL, PANEL), 1)
        left[0], left[1] = halves(jnp.where(r >= c, m_ref[...], 0.0))

    o_ref[...] = dot_halves(halves(s_ref[...]), (left[0], left[1]), 1, 1)

    @pl.when((top_ref[0] == 1) & (step < PANEL // per))
    def _():
        r, c = block((PANEL, LANES), 0), block((PANEL, LANES), 1)
        for half in range(PANEL // LANES):
            lanes = slice(LANES * half, LANES * half + LANES)
            inside = (r // BLOCK) == (c + LANES * half) // BLOCK
            upper = jnp.where(inside, u_ref[...], m_ref[:, lanes])
            upper = jnp.where(r <= c + LANES * half, upper, 0.0).T
            for s in range(LANES // per):
                @pl.when(step == half * (LANES // per) + s)
                def _():
                    o_ref[...] = upper[per * s : per * s + per]


def finish(top, rows, m, u):
    width, per = rows.shape[0], 128
    whole = lambda x: pl.BlockSpec(x.shape, lambda i: (0, 0))
    return pl.pallas_call(
        finish_body,
        name="finish",
        compiler_params=PARAMS,
        grid=(width // per,),
        out_shape=f32(width, PANEL),
        in_specs=[
            pl.BlockSpec(memory_space=pltpu.SMEM),
            pl.BlockSpec((per, PANEL), lambda i: (i, 0)),
            whole(m),
            whole(u),
        ],
        out_specs=pl.BlockSpec((per, PANEL), lambda i: (i, 0)),
        scratch_shapes=[pltpu.VMEM((2, PANEL, PANEL), jnp.bfloat16)],
        cost_estimate=pl.CostEstimate(
            flops=2 * width * PANEL * PANEL, bytes_accessed=8 * width * PANEL, transcendentals=0
        ),
    )(top, rows, m, u)


def shards(sizes, coupling, inverse_slabs, barrier_diagonal):
    n_zh, n_x, n_core, n_y, n_zl = (sizes[a] for a in AXES)
    n_xc, n_z = n_x * n_core, n_zh * n_zl
    own = coupling[0]
    depth, width = own.shape
    y, zl = lax.axis_index("y"), lax.axis_index("zl")
    swap = functools.partial(lax.all_to_all, split_axis=0, concat_axis=0)

    per = depth // n_y
    cut = lambda k: own[per * k : per * k + per, :PANEL]
    parts = []
    for k in range(1, n_y):
        parts.append(lax.ppermute(cut(k), ("y", "zl"), [(0, k * n_zl)]))
    inv = swap(copies(n_zl, inverse_slabs[0]), "zl").reshape(-1, depth)
    inv = swap(copies(n_y, inv), "y").reshape(depth, depth)
    first = jnp.where((y == 0) & (zl == 0), cut(0), 0.0)
    mine = call(sum_body, f32(per, PANEL), first, *parts)
    step = n_zl // 2
    while step:
        pairs = [(j, j + step) for j in range(0, n_zl, 2 * step)]
        got = lax.ppermute(mine, "zl", pairs)
        if step > 1:
            mine = mine + got
        step //= 2
    panel = swap(copies(n_y, mine, got), "y").reshape(depth, PANEL)

    turned = call(turn_body, bf16(2, width, depth), coupling, flops=2 * 10**9)
    n_row, n_piv = width // n_xc, 3 * PANEL // 4 // n_xc
    terms = multiply(turned, inv, panel, n_xc)
    terms = swap(terms, ("x", "core"))
    rows, pivot = call(total_body, [f32(n_row, PANEL), f32(n_piv, PANEL)], terms)

    half = n_zl // 2
    flip = [(z, (z + (half if z // half % 2 else -half)) % n_z) for z in range(n_z)]
    other = lax.ppermute(pivot, ("zh", "zl"), flip)
    pivot = swap(copies(n_xc, pivot, other), ("x", "core")).reshape(-1, PANEL)
    other = lax.ppermute(rows, "zh", [(0, 1), (1, 0)])
    rows = swap(copies(n_xc, rows, other), ("x", "core")).reshape(width, PANEL)

    m, u = call(
        factor_body, [f32(PANEL, PANEL), f32(PANEL, LANES)],
        pivot, barrier_diagonal[:PANEL].reshape(1, PANEL),
        flops=6 * 10**9,
    )
    top = ((y == 0) & (zl == 0)).astype(jnp.int32).reshape(1)
    return finish(top, rows, m, u)


def solution(mesh):
    sizes = {"zh": 2, "x": 4, "core": 2, "y": 4, "zl": 8}
    fine = Mesh(mesh.devices.reshape([sizes[a] for a in AXES]), AXES)
    return jax.shard_map(
        functools.partial(shards, sizes),
        mesh=fine,
        in_specs=(
            P(("zh", "x", "core"), None, ("y", "zl")),
            P(("zh", "x", "core"), ("y", "zl"), None),
            P(),
        ),
        out_specs=P(("y", "zl"), None),
        check_vma=False,
    )
```

```python
import functools

import jax
import jax.numpy as jnp
from jax import lax
from jax.experimental import pallas as pl
from jax.experimental.pallas import tpu as pltpu
from jax.sharding import Mesh, PartitionSpec as P

PANEL = 256
BLOCK = 64
LANES = 128
AXES = ("zh", "x", "core", "y", "zl")
HIGHEST = lax.Precision.HIGHEST
VMEM = pl.BlockSpec(memory_space=pltpu.VMEM)
PARAMS = pltpu.CompilerParams(vmem_limit_bytes=12 << 20)


def f32(*shape):
    return jax.ShapeDtypeStruct(shape, jnp.float32)


def bf16(*shape):
    return jax.ShapeDtypeStruct(shape, jnp.bfloat16)


def dot(a, b, da, db):
    return lax.dot_general(
        a, b, (((da,), (db,)), ((), ())), precision=HIGHEST, preferred_element_type=jnp.float32
    )


def call(body, outs, *args, flops=0, scalars=0):
    size = sum(a.size for a in args) * 4
    smem = pl.BlockSpec(memory_space=pltpu.SMEM)
    return pl.pallas_call(
        body,
        compiler_params=PARAMS,
        out_shape=outs,
        in_specs=[smem] * scalars + [VMEM] * (len(args) - scalars),
        out_specs=jax.tree.map(lambda _: VMEM, outs),
        cost_estimate=pl.CostEstimate(flops=flops, bytes_accessed=size, transcendentals=0),
    )(*args)


def lane_of(x, c): return jnp.broadcast_to(x[:, c:c+1], (8, LANES))


def row_of(x, r): return jnp.broadcast_to(x[r:r+1, :], (8, LANES))


def base(tiles, lane0):
    row = lax.broadcasted_iota(jnp.int32, (8, LANES), 0)
    n = len(tiles)
    for s in range(n):
        x = tiles[s]
        cols = [lane_of(x, lane0 + 8*s + j) for j in range(8)]
        rest = [[lane_of(tiles[t], lane0 + 8*s + j) for j in range(8)] for t in range(s+1, n)]
        done = None
        for j in range(8):
            rs = lax.rsqrt(row_of(cols[j], j))
            u = row_of(x, j)
            scaled = u * rs
            g = scaled * rs
            done = scaled if done is None else jnp.where(row >= j, scaled, done)
            x = jnp.where(row == j, g, x - cols[j] * g)
            for l in range(j+1, 8):
                cl = row_of(cols[l], j) * (rs * rs)
                cols[l] = jnp.where(row == j, cl, cols[l] - cols[j] * cl)
        tiles[s] = done
        gs = [row_of(x, j) for j in range(8)]
        for i, t in enumerate(range(s+1, n)):
            acc = tiles[t]
            for j in range(8): acc = acc - rest[i][j] * gs[j]
            tiles[t] = acc
    return tiles


def factor_body(core_ref, mine_ref, other_ref, diag_ref, m_ref, u_ref):
    half = PANEL // 2
    r = lax.broadcasted_iota(jnp.int32, (half, PANEL), 0)
    c = lax.broadcasted_iota(jnp.int32, (half, PANEL), 1)
    diag = diag_ref[...]
    mine, other, first = mine_ref[...], other_ref[...], core_ref[0] == 0
    p = jnp.concatenate(
        [jnp.where(first, mine, other), jnp.where(first, other, mine)], axis=0
    )
    m_ref[:half] = p[:half] + jnp.where(r == c, diag, 0.0)
    last = p[half:]
    last = jnp.concatenate([last[:, :half], last[:, half:]], axis=0)
    last = jnp.concatenate([jnp.zeros_like(last), last], axis=1)
    m_ref[half:] = last + jnp.where(r + half == c, diag, 0.0)
    lane = lax.broadcasted_iota(jnp.int32, (BLOCK, LANES), 1)
    sub = lax.broadcasted_iota(jnp.int32, (BLOCK, LANES), 0)
    wlane = lax.broadcasted_iota(jnp.int32, (BLOCK, PANEL), 1)
    wsub = lax.broadcasted_iota(jnp.int32, (BLOCK, PANEL), 0)
    for k in range(PANEL // BLOCK):
        odd = k % 2
        seg = m_ref[BLOCK*k:BLOCK*k+BLOCK, LANES*(k//2):LANES*(k//2)+LANES]
        eye = (lane == sub + BLOCK*(1-odd)).astype(jnp.float32)
        own = (lane // BLOCK) == odd
        x = jnp.where(own, seg, eye)
        tiles = base([x[8*t:8*t+8] for t in range(BLOCK//8)], BLOCK*odd)
        x = jnp.concatenate(tiles, axis=0)
        u_ref[BLOCK*k:BLOCK*k+BLOCK, :] = x
        left = jnp.where(own, 0.0, x)
        mrow = m_ref[BLOCK*k:BLOCK*k+BLOCK, :]
        mrow = jnp.where(wlane // BLOCK == k, (wlane == wsub + BLOCK*k).astype(jnp.float32), mrow)
        z = jnp.zeros((BLOCK, PANEL), jnp.float32)
        rhs = jnp.concatenate([mrow, z] if odd else [z, mrow], axis=0)
        nk = lax.dot_general(left, rhs, (((1,),(0,)),((),())), precision=HIGHEST, preferred_element_type=jnp.float32)
        m_ref[BLOCK*k:BLOCK*k+BLOCK, :] = nk
        if k + 1 < PANEL // BLOCK:
            upd = lax.dot_general(nk, nk, (((0,),(0,)),((),())), precision=HIGHEST, preferred_element_type=jnp.float32)
            lo = BLOCK*(k+1)
            below = m_ref[lo:, :]
            wl = lax.broadcasted_iota(jnp.int32, below.shape, 1)
            m_ref[lo:, :] = jnp.where(wl // BLOCK == k, 0.0, below) - upd[lo:, :]


def sum_body(*refs):
    *ins, out = refs
    total = ins[0][...]
    for ref in ins[1:]:
        total = total + ref[...]
    out[...] = total


def copies_body(*refs):
    *ins, out = refs
    total = ins[0][...]
    for ref in ins[1:]:
        total = total + ref[...]
    for i in range(out.shape[0]):
        out[i] = total


def copies(n, *parts):
    return call(copies_body, f32(n, *parts[0].shape), *parts)


def solve_body(first_ref, second_ref, panel_ref, o_ref):
    panel = panel_ref[...]
    half = first_ref.shape[0]
    for at, ref in ((0, first_ref), (half, second_ref)):
        rows = dot(ref[...], panel, 1, 0)
        for i in range(o_ref.shape[0]):
            o_ref[i, at : at + half] = rows


def total_body(x_ref, *outs):
    at = 0
    for out in outs:
        rows = slice(at, at + out.shape[0])
        total = x_ref[0, rows]
        for i in range(1, x_ref.shape[0]):
            total = total + x_ref[i, rows]
        out[...] = total
        at += out.shape[0]


def halves(x):
    high = x.astype(jnp.bfloat16)
    return high, (x - high.astype(jnp.float32)).astype(jnp.bfloat16)


def dot_halves(a, b, da, db):
    one = lambda p, q: lax.dot_general(
        p, q, (((da,), (db,)), ((), ())), preferred_element_type=jnp.float32
    )
    return one(a[0], b[0]) + (one(a[0], b[1]) + one(a[1], b[0]))


def turn_body(masks, zl_ref, own_ref, panel_ref, high_ref, low_ref):
    per = own_ref.shape[1] // (4 * len(masks))
    starts = [
        pl.multiple_of((y * len(masks) + (zl_ref[0] ^ mask)) * per, per)
        for y in range(4)
        for mask in masks
    ]
    own = jnp.concatenate([own_ref[0, pl.ds(s, per)] for s in starts], axis=0)
    panel = jnp.concatenate([panel_ref[pl.ds(s, per)] for s in starts], axis=0)
    at = 0
    for x in (own, panel):
        rows = slice(at, at + x.shape[1])
        high_ref[rows], low_ref[rows] = halves(x.T)
        at += x.shape[1]


def terms_body(core_ref, high_ref, solved_ref, low_ref, keep_ref, send_ref, low, sem):
    fetch = pltpu.make_async_copy(low_ref, low, sem)
    fetch.start()
    width, half = high_ref.shape[0] - PANEL, PANEL // 2
    first = core_ref[0] == 0
    one = lambda a, b: jnp.dot(a, b, preferred_element_type=jnp.float32)
    s = halves(solved_ref[...])
    x = one(high_ref[...], s[0]) + one(high_ref[...], s[1])
    fetch.wait()
    x = x + one(low[...], s[0])
    rows, x = x[:width], x[width:]
    last = jnp.concatenate(
        [x[half : half + half // 2, half:], x[half + half // 2 :, half:]], axis=1
    )
    x = jnp.concatenate([x[:half], last], axis=0)
    piv = x.shape[0] // 2
    at = keep_ref.shape[0] - piv
    keep_ref[at:] = jnp.where(first, x[:piv], x[piv:])
    send_ref[at:] = jnp.where(first, x[piv:], x[:piv])
    x = rows.reshape(4, 2, at // 4, PANEL)
    keep_ref[:at] = jnp.where(first, x[:, 0], x[:, 1]).reshape(at, PANEL)
    send_ref[:at] = jnp.where(first, x[:, 1], x[:, 0]).reshape(at, PANEL)


def multiply(core, high, low, solved, rows):
    return pl.pallas_call(
        terms_body,
        name="terms",
        out_shape=[f32(rows, PANEL)] * 2,
        compiler_params=PARAMS,
        in_specs=[
            pl.BlockSpec(memory_space=pltpu.SMEM), VMEM, VMEM,
            pl.BlockSpec(memory_space=pltpu.HBM),
        ],
        out_specs=[VMEM] * 2,
        scratch_shapes=[pltpu.VMEM(low.shape, low.dtype), pltpu.SemaphoreType.DMA],
        cost_estimate=pl.CostEstimate(
            flops=6 * high.size * PANEL, bytes_accessed=4 * high.size, transcendentals=0
        ),
    )(core, high, solved, pltpu.with_memory_space_constraint(low, pltpu.HBM))


def share_body(keep_ref, other_ref, o_ref):
    n = o_ref.shape[0]
    total = keep_ref[...] + other_ref[...]
    rows = (total.shape[0] - PANEL * 3 // 8) // n
    for i in range(n):
        o_ref[i, :rows] = total[rows * i : rows * i + rows]
        o_ref[i, rows:] = total[rows * n :]


def finish_body(top_ref, s_ref, m_ref, u_ref, o_ref, left):
    step, per = pl.program_id(0), s_ref.shape[0]
    block = lambda shape, d: lax.broadcasted_iota(jnp.int32, shape, d)

    @pl.when(step == 0)
    def _():
        r, c = block((PANEL, PANEL), 0), block((PANEL, PANEL), 1)
        left[0], left[1] = halves(jnp.where(r >= c, m_ref[...], 0.0))

    o_ref[...] = dot_halves(halves(s_ref[...]), (left[0], left[1]), 1, 1)

    @pl.when((top_ref[0] == 1) & (step < PANEL // per))
    def _():
        r, c = block((PANEL, LANES), 0), block((PANEL, LANES), 1)
        for half in range(PANEL // LANES):
            lanes = slice(LANES * half, LANES * half + LANES)
            inside = (r // BLOCK) == (c + LANES * half) // BLOCK
            upper = jnp.where(inside, u_ref[...], m_ref[:, lanes])
            upper = jnp.where(r <= c + LANES * half, upper, 0.0).T
            for s in range(LANES // per):
                @pl.when(step == half * (LANES // per) + s)
                def _():
                    o_ref[...] = upper[per * s : per * s + per]


def finish(top, rows, m, u):
    width, per = rows.shape[0], 128
    whole = lambda x: pl.BlockSpec(x.shape, lambda i: (0, 0))
    return pl.pallas_call(
        finish_body,
        name="finish",
        compiler_params=PARAMS,
        grid=(width // per,),
        out_shape=f32(width, PANEL),
        in_specs=[
            pl.BlockSpec(memory_space=pltpu.SMEM),
            pl.BlockSpec((per, PANEL), lambda i: (i, 0)),
            whole(m),
            whole(u),
        ],
        out_specs=pl.BlockSpec((per, PANEL), lambda i: (i, 0)),
        scratch_shapes=[pltpu.VMEM((2, PANEL, PANEL), jnp.bfloat16)],
        cost_estimate=pl.CostEstimate(
            flops=2 * width * PANEL * PANEL, bytes_accessed=8 * width * PANEL, transcendentals=0
        ),
    )(top, rows, m, u)


def shards(sizes, coupling, inverse_slabs, barrier_diagonal):
    n_zh, n_x, n_core, n_y, n_zl = (sizes[a] for a in AXES)
    n_xc, n_z = n_x * n_core, n_zh * n_zl
    own = coupling[0]
    depth, width = own.shape
    y, zl = lax.axis_index("y"), lax.axis_index("zl")
    swap = functools.partial(lax.all_to_all, split_axis=0, concat_axis=0)

    per = depth // n_y
    cut = lambda k: own[per * k : per * k + per, :PANEL]
    parts = []
    for k in range(1, n_y):
        parts.append(lax.ppermute(cut(k), ("y", "zl"), [(0, k * n_zl)]))
    first = jnp.where((y == 0) & (zl == 0), cut(0), 0.0)
    inv, masks = inverse_slabs[0], [0]
    mine, step = None, n_zl // 2
    while step:
        far = lax.ppermute(inv, "zl", [(z, z ^ step) for z in range(n_zl)])
        if mine is None:
            mine = call(sum_body, f32(per, PANEL), first, *parts)
        pairs = [(z, z + step) for z in range(0, n_zl, 2 * step)]
        got = lax.ppermute(mine, "zl", pairs)
        masks = masks + [m ^ step for m in masks]
        if step > 1:
            mine = mine + got
            inv = jnp.concatenate([inv, far], axis=0)
        step //= 2
    panel = swap(copies(n_y, mine, got), "y").reshape(depth, PANEL)

    solved = call(
        solve_body, f32(n_y, per, PANEL), inv, far, panel,
        flops=2 * per * depth * PANEL,
    )
    solved = swap(solved, "y").reshape(depth, PANEL)
    one = lambda i: i.astype(jnp.int32).reshape(1)
    core = one(lax.axis_index("core"))
    high, low = call(
        functools.partial(turn_body, masks), [bf16(width + PANEL, depth)] * 2,
        one(zl), coupling, panel, flops=10**9, scalars=1,
    )

    n_row, n_piv = width // n_xc, 3 * PANEL // 8
    keep, send = multiply(core, high, low, solved, n_x * n_row + n_piv)
    other_core = [(0, 1), (1, 0)]
    other = lax.ppermute(send, "core", other_core)
    terms = call(share_body, f32(n_x, n_row + n_piv, PANEL), keep, other)
    terms = swap(terms, "x")
    rows, pivot = call(total_body, [f32(n_row, PANEL), f32(n_piv, PANEL)], terms)

    half = n_zl // 2
    flip = [(z, (z + (half if z // half % 2 else -half)) % n_z) for z in range(n_z)]
    pivot = pivot + lax.ppermute(pivot, ("zh", "zl"), flip)
    other_pivot = lax.ppermute(pivot, "core", other_core)
    other = lax.ppermute(rows, "zh", [(0, 1), (1, 0)])
    rows = swap(copies(n_xc, rows, other), ("x", "core")).reshape(width, PANEL)

    m, u = call(
        factor_body, [f32(PANEL, PANEL), f32(PANEL, LANES)],
        core, pivot, other_pivot, barrier_diagonal[:PANEL].reshape(1, PANEL),
        flops=6 * 10**9, scalars=1,
    )
    top = one((y == 0) & (zl == 0))
    return finish(top, rows, m, u)


def solution(mesh):
    sizes = {"zh": 2, "x": 4, "core": 2, "y": 4, "zl": 8}
    fine = Mesh(mesh.devices.reshape([sizes[a] for a in AXES]), AXES)
    return jax.shard_map(
        functools.partial(shards, sizes),
        mesh=fine,
        in_specs=(
            P(("zh", "x", "core"), None, ("y", "zl")),
            P(("zh", "x", "core"), ("y", "zl"), None),
            P(),
        ),
        out_specs=P(("y", "zl"), None),
        check_vma=False,
    )
```

```python
import functools

import jax
import jax.numpy as jnp
from jax import lax
from jax.experimental import pallas as pl
from jax.experimental.pallas import tpu as pltpu
from jax.sharding import Mesh, PartitionSpec as P

PANEL = 256
BLOCK = 64
LANES = 128
PACKED = 160
AXES = ("zh", "x", "core", "y", "zl")
HIGHEST = lax.Precision.HIGHEST
VMEM = pl.BlockSpec(memory_space=pltpu.VMEM)
PARAMS = pltpu.CompilerParams(vmem_limit_bytes=12 << 20)


def f32(*shape):
    return jax.ShapeDtypeStruct(shape, jnp.float32)


def bf16(*shape):
    return jax.ShapeDtypeStruct(shape, jnp.bfloat16)


def dot(a, b, da, db):
    return lax.dot_general(
        a, b, (((da,), (db,)), ((), ())), precision=HIGHEST, preferred_element_type=jnp.float32
    )


def call(body, outs, *args, flops=0, scalars=0):
    size = sum(a.size for a in args) * 4
    smem = pl.BlockSpec(memory_space=pltpu.SMEM)
    return pl.pallas_call(
        body,
        compiler_params=PARAMS,
        out_shape=outs,
        in_specs=[smem] * scalars + [VMEM] * (len(args) - scalars),
        out_specs=jax.tree.map(lambda _: VMEM, outs),
        cost_estimate=pl.CostEstimate(flops=flops, bytes_accessed=size, transcendentals=0),
    )(*args)


def lane_of(x, c): return jnp.broadcast_to(x[:, c:c+1], (8, LANES))


def row_of(x, r): return jnp.broadcast_to(x[r:r+1, :], (8, LANES))


def base(tiles, lane0):
    row = lax.broadcasted_iota(jnp.int32, (8, LANES), 0)
    n = len(tiles)
    for s in range(n):
        x = tiles[s]
        cols = [lane_of(x, lane0 + 8*s + j) for j in range(8)]
        rest = [[lane_of(tiles[t], lane0 + 8*s + j) for j in range(8)] for t in range(s+1, n)]
        done = None
        for j in range(8):
            rs = lax.rsqrt(row_of(cols[j], j))
            u = row_of(x, j)
            scaled = u * rs
            g = scaled * rs
            done = scaled if done is None else jnp.where(row >= j, scaled, done)
            x = jnp.where(row == j, g, x - cols[j] * g)
            for l in range(j+1, 8):
                cl = row_of(cols[l], j) * (rs * rs)
                cols[l] = jnp.where(row == j, cl, cols[l] - cols[j] * cl)
        tiles[s] = done
        gs = [row_of(x, j) for j in range(8)]
        for i, t in enumerate(range(s+1, n)):
            acc = tiles[t]
            for j in range(8): acc = acc - rest[i][j] * gs[j]
            tiles[t] = acc
    return tiles


def factor_body(core_ref, mine_ref, other_ref, diag_ref, m_ref, u_ref):
    mine, other, first = mine_ref[...], other_ref[...], core_ref[0] == 0
    p = jnp.concatenate(
        [jnp.where(first, mine, other), jnp.where(first, other, mine)], axis=0
    )
    b = BLOCK
    third = p[2 * b :]
    third = jnp.concatenate([third[:, LANES:], third[:, :LANES]], axis=0)
    blocks = (p[:b], p[b : 2 * b], jnp.concatenate([third, third], axis=1))
    r = lax.broadcasted_iota(jnp.int32, (b, PANEL), 0)
    c = lax.broadcasted_iota(jnp.int32, (b, PANEL), 1)
    for i, rows in enumerate(blocks + (pltpu.roll(p[b : 2 * b], 3 * b, 1),)):
        m_ref[b * i : b * i + b] = rows + jnp.where(r + b * i == c, diag_ref[...], 0.0)
    lane = lax.broadcasted_iota(jnp.int32, (BLOCK, LANES), 1)
    sub = lax.broadcasted_iota(jnp.int32, (BLOCK, LANES), 0)
    wlane = lax.broadcasted_iota(jnp.int32, (BLOCK, PANEL), 1)
    wsub = lax.broadcasted_iota(jnp.int32, (BLOCK, PANEL), 0)
    for k in range(PANEL // BLOCK):
        odd = k % 2
        seg = m_ref[BLOCK*k:BLOCK*k+BLOCK, LANES*(k//2):LANES*(k//2)+LANES]
        eye = (lane == sub + BLOCK*(1-odd)).astype(jnp.float32)
        own = (lane // BLOCK) == odd
        x = jnp.where(own, seg, eye)
        tiles = base([x[8*t:8*t+8] for t in range(BLOCK//8)], BLOCK*odd)
        x = jnp.concatenate(tiles, axis=0)
        u_ref[BLOCK*k:BLOCK*k+BLOCK, :] = x
        left = jnp.where(own, 0.0, x)
        mrow = m_ref[BLOCK*k:BLOCK*k+BLOCK, :]
        mrow = jnp.where(wlane // BLOCK == k, (wlane == wsub + BLOCK*k).astype(jnp.float32), mrow)
        z = jnp.zeros((BLOCK, PANEL), jnp.float32)
        rhs = jnp.concatenate([mrow, z] if odd else [z, mrow], axis=0)
        nk = lax.dot_general(left, rhs, (((1,),(0,)),((),())), precision=HIGHEST, preferred_element_type=jnp.float32)
        m_ref[BLOCK*k:BLOCK*k+BLOCK, :] = nk
        if k + 1 < PANEL // BLOCK:
            upd = lax.dot_general(nk, nk, (((0,),(0,)),((),())), precision=HIGHEST, preferred_element_type=jnp.float32)
            lo = BLOCK*(k+1)
            below = m_ref[lo:, :]
            wl = lax.broadcasted_iota(jnp.int32, below.shape, 1)
            m_ref[lo:, :] = jnp.where(wl // BLOCK == k, 0.0, below) - upd[lo:, :]


def sum_body(*refs):
    *ins, out = refs
    total = ins[0][...]
    for ref in ins[1:]:
        total = total + ref[...]
    out[...] = total


def copies_body(*refs):
    *ins, out = refs
    total = ins[0][...]
    for ref in ins[1:]:
        total = total + ref[...]
    for i in range(out.shape[0]):
        out[i] = total


def copies(n, *parts):
    return call(copies_body, f32(n, *parts[0].shape), *parts)


def solve_body(y_ref, inv_ref, *refs):
    *parts, panel_ref, o_ref = refs
    per = parts[0].shape[0]
    for ahead, part in enumerate(parts):
        y = lax.rem(y_ref[0] + ahead, len(parts))
        panel_ref[pl.ds(pl.multiple_of(y * per, per), per)] = part[...]
    rows = dot(inv_ref[...], panel_ref[...], 1, 0)
    for i in range(o_ref.shape[0]):
        o_ref[i] = rows


def total_body(x_ref, *outs):
    at = 0
    for out in outs:
        rows = slice(at, at + out.shape[0])
        total = x_ref[0, rows]
        for i in range(1, x_ref.shape[0]):
            total = total + x_ref[i, rows]
        out[...] = total
        at += out.shape[0]


def halves(x):
    high = x.astype(jnp.bfloat16)
    return high, (x - high.astype(jnp.float32)).astype(jnp.bfloat16)


def dot_halves(a, b, da, db):
    one = lambda p, q: lax.dot_general(
        p, q, (((da,), (db,)), ((), ())), preferred_element_type=jnp.float32
    )
    return one(a[0], b[0]) + (one(a[0], b[1]) + one(a[1], b[0]))


def turn_body(own_ref, panel_ref, own_high, own_low, panel_high, panel_low):
    own_high[...], own_low[...] = halves(own_ref[0].T)
    panel_high[...], panel_low[...] = halves(panel_ref[...].T)


def terms_body(
    core_ref, own_high, panel_high, panel_low, solved_ref, low_ref, keep_ref, send_ref, low, sem
):
    fetch = pltpu.make_async_copy(low_ref, low, sem)
    fetch.start()
    s = halves(solved_ref[...])
    first = core_ref[0] == 0
    x = dot_halves((panel_high[...], panel_low[...]), s, 1, 0)
    b, w = BLOCK, LANES
    third = jnp.concatenate([x[2 * b + b // 2 : 3 * b, w:], x[2 * b : 2 * b + b // 2, w:]], axis=1)
    lane = lax.broadcasted_iota(jnp.int32, (b, PANEL), 1)
    second = jnp.where(lane < b, pltpu.roll(x[3 * b :], b, 1), x[b : 2 * b])
    x = jnp.concatenate([x[:b], second, third], axis=0)
    piv = x.shape[0] // 2
    at = keep_ref.shape[0] - piv
    keep_ref[at:] = jnp.where(first, x[:piv], x[piv:])
    send_ref[at:] = jnp.where(first, x[piv:], x[:piv])
    one = lambda a, b: jnp.dot(a, b, preferred_element_type=jnp.float32)
    x = one(own_high[...], s[0]) + one(own_high[...], s[1])
    fetch.wait()
    x = x + one(low[...], s[0])
    x = x.reshape(4, 2, at // 4, PANEL)
    keep_ref[:at] = jnp.where(first, x[:, 0], x[:, 1]).reshape(at, PANEL)
    send_ref[:at] = jnp.where(first, x[:, 1], x[:, 0]).reshape(at, PANEL)


def multiply(core, parts, solved, rows):
    high, low, *panels = parts
    return pl.pallas_call(
        terms_body,
        name="terms",
        out_shape=[f32(rows, PANEL)] * 2,
        compiler_params=PARAMS,
        in_specs=[
            pl.BlockSpec(memory_space=pltpu.SMEM), VMEM, VMEM, VMEM, VMEM,
            pl.BlockSpec(memory_space=pltpu.HBM),
        ],
        out_specs=[VMEM] * 2,
        scratch_shapes=[pltpu.VMEM(low.shape, low.dtype), pltpu.SemaphoreType.DMA],
        cost_estimate=pl.CostEstimate(
            flops=9 * high.size * PANEL, bytes_accessed=6 * high.size, transcendentals=0
        ),
    )(core, high, *panels, solved, pltpu.with_memory_space_constraint(low, pltpu.HBM))


def share_body(keep_ref, other_ref, o_ref):
    n = o_ref.shape[0]
    total = keep_ref[...] + other_ref[...]
    rows = (total.shape[0] - PACKED // 2) // n
    for i in range(n):
        o_ref[i, :rows] = total[rows * i : rows * i + rows]
        o_ref[i, rows:] = total[rows * n :]


def finish_body(top_ref, s_ref, m_ref, u_ref, o_ref, left):
    step, per = pl.program_id(0), s_ref.shape[0]
    block = lambda shape, d: lax.broadcasted_iota(jnp.int32, shape, d)

    @pl.when(step == 0)
    def _():
        r, c = block((PANEL, PANEL), 0), block((PANEL, PANEL), 1)
        left[0], left[1] = halves(jnp.where(r >= c, m_ref[...], 0.0))

    o_ref[...] = dot_halves(halves(s_ref[...]), (left[0], left[1]), 1, 1)

    @pl.when((top_ref[0] == 1) & (step < PANEL // per))
    def _():
        r, c = block((PANEL, LANES), 0), block((PANEL, LANES), 1)
        for half in range(PANEL // LANES):
            lanes = slice(LANES * half, LANES * half + LANES)
            inside = (r // BLOCK) == (c + LANES * half) // BLOCK
            upper = jnp.where(inside, u_ref[...], m_ref[:, lanes])
            upper = jnp.where(r <= c + LANES * half, upper, 0.0).T
            for s in range(LANES // per):
                @pl.when(step == half * (LANES // per) + s)
                def _():
                    o_ref[...] = upper[per * s : per * s + per]


def finish(top, rows, m, u):
    width, per = rows.shape[0], 128
    whole = lambda x: pl.BlockSpec(x.shape, lambda i: (0, 0))
    return pl.pallas_call(
        finish_body,
        name="finish",
        compiler_params=PARAMS,
        grid=(width // per,),
        out_shape=f32(width, PANEL),
        in_specs=[
            pl.BlockSpec(memory_space=pltpu.SMEM),
            pl.BlockSpec((per, PANEL), lambda i: (i, 0)),
            whole(m),
            whole(u),
        ],
        out_specs=pl.BlockSpec((per, PANEL), lambda i: (i, 0)),
        scratch_shapes=[pltpu.VMEM((2, PANEL, PANEL), jnp.bfloat16)],
        cost_estimate=pl.CostEstimate(
            flops=2 * width * PANEL * PANEL, bytes_accessed=8 * width * PANEL, transcendentals=0
        ),
    )(top, rows, m, u)


def shards(sizes, coupling, inverse_slabs, barrier_diagonal):
    n_zh, n_x, n_core, n_y, n_zl = (sizes[a] for a in AXES)
    n_xc, n_z = n_x * n_core, n_zh * n_zl
    own = coupling[0]
    depth, width = own.shape
    y, zl = lax.axis_index("y"), lax.axis_index("zl")
    swap = functools.partial(lax.all_to_all, split_axis=0, concat_axis=0)

    one = lambda i: i.astype(jnp.int32).reshape(1)
    per = depth // n_y
    cut = lambda k: own[per * k : per * k + per, :PANEL]
    parts = []
    for k in range(1, n_y):
        parts.append(lax.ppermute(cut(k), ("y", "zl"), [(0, k * n_zl)]))
    first = jnp.where((y == 0) & (zl == 0), cut(0), 0.0)
    mine = call(sum_body, f32(per, PANEL), first, *parts)
    step = n_zl // 2
    while step:
        pairs = [(z, z + step) for z in range(0, n_zl, 2 * step)]
        mine = mine + lax.ppermute(mine, "zl", pairs)
        step //= 2
    inv = swap(copies(n_zl, inverse_slabs[0]), "zl").reshape(per, depth)
    parts = [mine]
    for k in range(1, n_y):
        parts.append(lax.ppermute(mine, "y", [(i, (i - k) % n_y) for i in range(n_y)]))
    panel, solved = call(
        solve_body, [f32(depth, PANEL), f32(n_y, per, PANEL)], one(y), inv, *parts,
        flops=2 * per * depth * PANEL, scalars=1,
    )
    solved = swap(solved, "y").reshape(depth, PANEL)
    core = one(lax.axis_index("core"))
    parts = call(
        turn_body, [bf16(width, depth)] * 2 + [bf16(PANEL, depth)] * 2,
        coupling, panel, flops=10**9,
    )

    n_row, n_piv = width // n_xc, PACKED // 2
    keep, send = multiply(core, parts, solved, n_x * n_row + n_piv)
    other_core = [(0, 1), (1, 0)]
    other = lax.ppermute(send, "core", other_core)
    terms = call(share_body, f32(n_x, n_row + n_piv, PANEL), keep, other)
    terms = swap(terms, "x")
    rows, pivot = call(total_body, [f32(n_row, PANEL), f32(n_piv, PANEL)], terms)

    half = n_zl // 2
    flip = [(z, (z + (half if z // half % 2 else -half)) % n_z) for z in range(n_z)]
    pivot = pivot + lax.ppermute(pivot, ("zh", "zl"), flip)
    other_pivot = lax.ppermute(pivot, "core", other_core)
    other = lax.ppermute(rows, "zh", [(0, 1), (1, 0)])
    rows = swap(copies(n_xc, rows, other), ("x", "core")).reshape(width, PANEL)

    m, u = call(
        factor_body, [f32(PANEL, PANEL), f32(PANEL, LANES)],
        core, pivot, other_pivot, barrier_diagonal[:PANEL].reshape(1, PANEL),
        flops=6 * 10**9, scalars=1,
    )
    top = one((y == 0) & (zl == 0))
    return finish(top, rows, m, u)


def solution(mesh):
    sizes = {"zh": 2, "x": 4, "core": 2, "y": 4, "zl": 8}
    fine = Mesh(mesh.devices.reshape([sizes[a] for a in AXES]), AXES)
    return jax.shard_map(
        functools.partial(shards, sizes),
        mesh=fine,
        in_specs=(
            P(("zh", "x", "core"), None, ("y", "zl")),
            P(("zh", "x", "core"), ("y", "zl"), None),
            P(),
        ),
        out_specs=P(("y", "zl"), None),
        check_vma=False,
    )
```

```python
import functools

import jax
import jax.numpy as jnp
from jax import lax
from jax.experimental import pallas as pl
from jax.experimental.pallas import tpu as pltpu
from jax.sharding import Mesh, PartitionSpec as P

PANEL = 256
BLOCK = 64
LANES = 128
PACKED = 160
AXES = ("zh", "x", "core", "y", "zl")
HIGHEST = lax.Precision.HIGHEST
VMEM = pl.BlockSpec(memory_space=pltpu.VMEM)
PARAMS = pltpu.CompilerParams(vmem_limit_bytes=12 << 20)


def f32(*shape):
    return jax.ShapeDtypeStruct(shape, jnp.float32)


def bf16(*shape):
    return jax.ShapeDtypeStruct(shape, jnp.bfloat16)


def dot(a, b, da, db):
    return lax.dot_general(
        a, b, (((da,), (db,)), ((), ())), precision=HIGHEST, preferred_element_type=jnp.float32
    )


def call(body, outs, *args, flops=0, scalars=0):
    size = sum(a.size for a in args) * 4
    smem = pl.BlockSpec(memory_space=pltpu.SMEM)
    return pl.pallas_call(
        body,
        compiler_params=PARAMS,
        out_shape=outs,
        in_specs=[smem] * scalars + [VMEM] * (len(args) - scalars),
        out_specs=jax.tree.map(lambda _: VMEM, outs),
        cost_estimate=pl.CostEstimate(flops=flops, bytes_accessed=size, transcendentals=0),
    )(*args)


def lane_of(x, c): return jnp.broadcast_to(x[:, c:c+1], (8, LANES))


def row_of(x, r): return jnp.broadcast_to(x[r:r+1, :], (8, LANES))


def base(tiles, lane0):
    row = lax.broadcasted_iota(jnp.int32, (8, LANES), 0)
    n = len(tiles)
    for s in range(n):
        x = tiles[s]
        cols = [lane_of(x, lane0 + 8*s + j) for j in range(8)]
        rest = [[lane_of(tiles[t], lane0 + 8*s + j) for j in range(8)] for t in range(s+1, n)]
        done = None
        for j in range(8):
            rs = lax.rsqrt(row_of(cols[j], j))
            u = row_of(x, j)
            scaled = u * rs
            g = scaled * rs
            done = scaled if done is None else jnp.where(row >= j, scaled, done)
            x = jnp.where(row == j, g, x - cols[j] * g)
            for l in range(j+1, 8):
                cl = row_of(cols[l], j) * (rs * rs)
                cols[l] = jnp.where(row == j, cl, cols[l] - cols[j] * cl)
        tiles[s] = done
        gs = [row_of(x, j) for j in range(8)]
        for i, t in enumerate(range(s+1, n)):
            acc = tiles[t]
            for j in range(8): acc = acc - rest[i][j] * gs[j]
            tiles[t] = acc
    return tiles


def factor_body(core_ref, mine_ref, other_ref, diag_ref, m_ref, u_ref):
    mine, other, first = mine_ref[...], other_ref[...], core_ref[0] == 0
    p = jnp.concatenate(
        [jnp.where(first, mine, other), jnp.where(first, other, mine)], axis=0
    )
    b = BLOCK
    third = p[2 * b :]
    third = jnp.concatenate([third[:, LANES:], third[:, :LANES]], axis=0)
    blocks = (p[:b], p[b : 2 * b], jnp.concatenate([third, third], axis=1))
    r = lax.broadcasted_iota(jnp.int32, (b, PANEL), 0)
    c = lax.broadcasted_iota(jnp.int32, (b, PANEL), 1)
    for i, rows in enumerate(blocks + (pltpu.roll(p[b : 2 * b], 3 * b, 1),)):
        m_ref[b * i : b * i + b] = rows + jnp.where(r + b * i == c, diag_ref[...], 0.0)
    lane = lax.broadcasted_iota(jnp.int32, (BLOCK, LANES), 1)
    sub = lax.broadcasted_iota(jnp.int32, (BLOCK, LANES), 0)
    wlane = lax.broadcasted_iota(jnp.int32, (BLOCK, PANEL), 1)
    wsub = lax.broadcasted_iota(jnp.int32, (BLOCK, PANEL), 0)
    for k in range(PANEL // BLOCK):
        odd = k % 2
        seg = m_ref[BLOCK*k:BLOCK*k+BLOCK, LANES*(k//2):LANES*(k//2)+LANES]
        eye = (lane == sub + BLOCK*(1-odd)).astype(jnp.float32)
        own = (lane // BLOCK) == odd
        x = jnp.where(own, seg, eye)
        tiles = base([x[8*t:8*t+8] for t in range(BLOCK//8)], BLOCK*odd)
        x = jnp.concatenate(tiles, axis=0)
        u_ref[BLOCK*k:BLOCK*k+BLOCK, :] = x
        left = jnp.where(own, 0.0, x)
        mrow = m_ref[BLOCK*k:BLOCK*k+BLOCK, :]
        mrow = jnp.where(wlane // BLOCK == k, (wlane == wsub + BLOCK*k).astype(jnp.float32), mrow)
        z = jnp.zeros((BLOCK, PANEL), jnp.float32)
        rhs = jnp.concatenate([mrow, z] if odd else [z, mrow], axis=0)
        nk = lax.dot_general(left, rhs, (((1,),(0,)),((),())), precision=HIGHEST, preferred_element_type=jnp.float32)
        m_ref[BLOCK*k:BLOCK*k+BLOCK, :] = nk
        if k + 1 < PANEL // BLOCK:
            upd = lax.dot_general(nk, nk, (((0,),(0,)),((),())), precision=HIGHEST, preferred_element_type=jnp.float32)
            lo = BLOCK*(k+1)
            below = m_ref[lo:, :]
            wl = lax.broadcasted_iota(jnp.int32, below.shape, 1)
            m_ref[lo:, :] = jnp.where(wl // BLOCK == k, 0.0, below) - upd[lo:, :]


def sum_body(*refs):
    *ins, out = refs
    total = ins[0][...]
    for ref in ins[1:]:
        total = total + ref[...]
    out[...] = total


def copies_body(*refs):
    *ins, out = refs
    total = ins[0][...]
    for ref in ins[1:]:
        total = total + ref[...]
    for i in range(out.shape[0]):
        out[i] = total


def copies(n, *parts):
    return call(copies_body, f32(n, *parts[0].shape), *parts)


def solve_body(masks, zl_ref, first_ref, second_ref, panel_ref, o_ref):
    panel = panel_ref[...]
    per = 2 * first_ref.shape[0] // len(masks)
    blocks = []
    for ref in (first_ref, second_ref):
        rows = dot(ref[...], panel, 1, 0)
        blocks += [rows[at : at + per] for at in range(0, rows.shape[0], per)]
    for mask, block in zip(masks, blocks):
        at = pl.ds(pl.multiple_of((zl_ref[0] ^ mask) * per, per), per)
        for i in range(o_ref.shape[0]):
            o_ref[i, at] = block


def total_body(x_ref, *outs):
    at = 0
    for out in outs:
        rows = slice(at, at + out.shape[0])
        total = x_ref[0, rows]
        for i in range(1, x_ref.shape[0]):
            total = total + x_ref[i, rows]
        out[...] = total
        at += out.shape[0]


def halves(x):
    high = x.astype(jnp.bfloat16)
    return high, (x - high.astype(jnp.float32)).astype(jnp.bfloat16)


def dot_halves(a, b, da, db):
    one = lambda p, q: lax.dot_general(
        p, q, (((da,), (db,)), ((), ())), preferred_element_type=jnp.float32
    )
    return one(a[0], b[0]) + (one(a[0], b[1]) + one(a[1], b[0]))


def turn_body(own_ref, panel_ref, own_high, own_low, panel_high, panel_low):
    own_high[...], own_low[...] = halves(own_ref[0].T)
    panel_high[...], panel_low[...] = halves(panel_ref[...].T)


def terms_body(
    core_ref, own_high, panel_high, panel_low, solved_ref, low_ref, keep_ref, send_ref, low, sem
):
    fetch = pltpu.make_async_copy(low_ref, low, sem)
    fetch.start()
    s = halves(solved_ref[...])
    first = core_ref[0] == 0
    x = dot_halves((panel_high[...], panel_low[...]), s, 1, 0)
    b, w = BLOCK, LANES
    third = jnp.concatenate([x[2 * b + b // 2 : 3 * b, w:], x[2 * b : 2 * b + b // 2, w:]], axis=1)
    lane = lax.broadcasted_iota(jnp.int32, (b, PANEL), 1)
    second = jnp.where(lane < b, pltpu.roll(x[3 * b :], b, 1), x[b : 2 * b])
    x = jnp.concatenate([x[:b], second, third], axis=0)
    piv = x.shape[0] // 2
    at = keep_ref.shape[0] - piv
    keep_ref[at:] = jnp.where(first, x[:piv], x[piv:])
    send_ref[at:] = jnp.where(first, x[piv:], x[:piv])
    one = lambda a, b: jnp.dot(a, b, preferred_element_type=jnp.float32)
    x = one(own_high[...], s[0]) + one(own_high[...], s[1])
    fetch.wait()
    x = x + one(low[...], s[0])
    x = x.reshape(4, 2, at // 4, PANEL)
    keep_ref[:at] = jnp.where(first, x[:, 0], x[:, 1]).reshape(at, PANEL)
    send_ref[:at] = jnp.where(first, x[:, 1], x[:, 0]).reshape(at, PANEL)


def multiply(core, parts, solved, rows):
    high, low, *panels = parts
    return pl.pallas_call(
        terms_body,
        name="terms",
        out_shape=[f32(rows, PANEL)] * 2,
        compiler_params=PARAMS,
        in_specs=[
            pl.BlockSpec(memory_space=pltpu.SMEM), VMEM, VMEM, VMEM, VMEM,
            pl.BlockSpec(memory_space=pltpu.HBM),
        ],
        out_specs=[VMEM] * 2,
        scratch_shapes=[pltpu.VMEM(low.shape, low.dtype), pltpu.SemaphoreType.DMA],
        cost_estimate=pl.CostEstimate(
            flops=9 * high.size * PANEL, bytes_accessed=6 * high.size, transcendentals=0
        ),
    )(core, high, *panels, solved, pltpu.with_memory_space_constraint(low, pltpu.HBM))


def share_body(keep_ref, other_ref, o_ref):
    n = o_ref.shape[0]
    total = keep_ref[...] + other_ref[...]
    rows = (total.shape[0] - PACKED // 2) // n
    for i in range(n):
        o_ref[i, :rows] = total[rows * i : rows * i + rows]
        o_ref[i, rows:] = total[rows * n :]


def finish_body(top_ref, s_ref, m_ref, u_ref, o_ref, left):
    step, per = pl.program_id(0), s_ref.shape[0]
    block = lambda shape, d: lax.broadcasted_iota(jnp.int32, shape, d)

    @pl.when(step == 0)
    def _():
        r, c = block((PANEL, PANEL), 0), block((PANEL, PANEL), 1)
        left[0], left[1] = halves(jnp.where(r >= c, m_ref[...], 0.0))

    o_ref[...] = dot_halves(halves(s_ref[...]), (left[0], left[1]), 1, 1)

    @pl.when((top_ref[0] == 1) & (step < PANEL // per))
    def _():
        r, c = block((PANEL, LANES), 0), block((PANEL, LANES), 1)
        for half in range(PANEL // LANES):
            lanes = slice(LANES * half, LANES * half + LANES)
            inside = (r // BLOCK) == (c + LANES * half) // BLOCK
            upper = jnp.where(inside, u_ref[...], m_ref[:, lanes])
            upper = jnp.where(r <= c + LANES * half, upper, 0.0).T
            for s in range(LANES // per):
                @pl.when(step == half * (LANES // per) + s)
                def _():
                    o_ref[...] = upper[per * s : per * s + per]


def finish(top, rows, m, u):
    width, per = rows.shape[0], 128
    whole = lambda x: pl.BlockSpec(x.shape, lambda i: (0, 0))
    return pl.pallas_call(
        finish_body,
        name="finish",
        compiler_params=PARAMS,
        grid=(width // per,),
        out_shape=f32(width, PANEL),
        in_specs=[
            pl.BlockSpec(memory_space=pltpu.SMEM),
            pl.BlockSpec((per, PANEL), lambda i: (i, 0)),
            whole(m),
            whole(u),
        ],
        out_specs=pl.BlockSpec((per, PANEL), lambda i: (i, 0)),
        scratch_shapes=[pltpu.VMEM((2, PANEL, PANEL), jnp.bfloat16)],
        cost_estimate=pl.CostEstimate(
            flops=2 * width * PANEL * PANEL, bytes_accessed=8 * width * PANEL, transcendentals=0
        ),
    )(top, rows, m, u)


def shards(sizes, coupling, inverse_slabs, barrier_diagonal):
    n_zh, n_x, n_core, n_y, n_zl = (sizes[a] for a in AXES)
    n_xc, n_z = n_x * n_core, n_zh * n_zl
    own = coupling[0]
    depth, width = own.shape
    y, zl = lax.axis_index("y"), lax.axis_index("zl")
    swap = functools.partial(lax.all_to_all, split_axis=0, concat_axis=0)

    one = lambda i: i.astype(jnp.int32).reshape(1)
    per = depth // n_y
    cut = lambda k: own[per * k : per * k + per, :PANEL]
    steps = [n_zl >> i for i in range(1, n_zl.bit_length())]
    inv, masks = inverse_slabs[0], [0]
    for step in steps:
        far = lax.ppermute(inv, "zl", [(z, z ^ step) for z in range(n_zl)])
        masks = masks + [m ^ step for m in masks]
        if step > 1:
            inv = jnp.concatenate([inv, far], axis=0)
    parts = []
    for k in range(1, n_y):
        parts.append(lax.ppermute(cut(k), ("y", "zl"), [(0, k * n_zl)]))
    first = jnp.where((y == 0) & (zl == 0), cut(0), 0.0)
    mine = call(sum_body, f32(per, PANEL), first, *parts)
    for step in steps:
        pairs = [(z, z + step) for z in range(0, n_zl, 2 * step)]
        got = lax.ppermute(mine, "zl", pairs)
        if step > 1:
            mine = mine + got
    panel = swap(copies(n_y, mine, got), "y").reshape(depth, PANEL)
    solved = call(
        functools.partial(solve_body, masks), f32(n_y, per, PANEL),
        one(zl), inv, far, panel, flops=2 * per * depth * PANEL, scalars=1,
    )
    solved = swap(solved, "y").reshape(depth, PANEL)
    core = one(lax.axis_index("core"))
    parts = call(
        turn_body, [bf16(width, depth)] * 2 + [bf16(PANEL, depth)] * 2,
        coupling, panel, flops=10**9,
    )

    n_row, n_piv = width // n_xc, PACKED // 2
    keep, send = multiply(core, parts, solved, n_x * n_row + n_piv)
    other_core = [(0, 1), (1, 0)]
    other = lax.ppermute(send, "core", other_core)
    terms = call(share_body, f32(n_x, n_row + n_piv, PANEL), keep, other)
    terms = swap(terms, "x")
    rows, pivot = call(total_body, [f32(n_row, PANEL), f32(n_piv, PANEL)], terms)

    half = n_zl // 2
    flip = [(z, (z + (half if z // half % 2 else -half)) % n_z) for z in range(n_z)]
    pivot = pivot + lax.ppermute(pivot, ("zh", "zl"), flip)
    other_pivot = lax.ppermute(pivot, "core", other_core)
    other = lax.ppermute(rows, "zh", [(0, 1), (1, 0)])
    rows = swap(copies(n_xc, rows, other), ("x", "core")).reshape(width, PANEL)

    m, u = call(
        factor_body, [f32(PANEL, PANEL), f32(PANEL, LANES)],
        core, pivot, other_pivot, barrier_diagonal[:PANEL].reshape(1, PANEL),
        flops=6 * 10**9, scalars=1,
    )
    top = one((y == 0) & (zl == 0))
    return finish(top, rows, m, u)


def solution(mesh):
    sizes = {"zh": 2, "x": 4, "core": 2, "y": 4, "zl": 8}
    fine = Mesh(mesh.devices.reshape([sizes[a] for a in AXES]), AXES)
    return jax.shard_map(
        functools.partial(shards, sizes),
        mesh=fine,
        in_specs=(
            P(("zh", "x", "core"), None, ("y", "zl")),
            P(("zh", "x", "core"), ("y", "zl"), None),
            P(),
        ),
        out_specs=P(("y", "zl"), None),
        check_vma=False,
    )
```

```python
import functools

import jax
import jax.numpy as jnp
from jax import lax
from jax.experimental import pallas as pl
from jax.experimental.pallas import tpu as pltpu
from jax.sharding import Mesh, PartitionSpec as P

PANEL = 256
BLOCK = 64
LANES = 128
PACKED = 160
AXES = ("zh", "x", "core", "y", "zl")
HIGHEST = lax.Precision.HIGHEST
VMEM = pl.BlockSpec(memory_space=pltpu.VMEM)
PARAMS = pltpu.CompilerParams(vmem_limit_bytes=12 << 20)


def f32(*shape):
    return jax.ShapeDtypeStruct(shape, jnp.float32)


def bf16(*shape):
    return jax.ShapeDtypeStruct(shape, jnp.bfloat16)


def dot(a, b, da, db):
    return lax.dot_general(
        a, b, (((da,), (db,)), ((), ())), precision=HIGHEST, preferred_element_type=jnp.float32
    )


def call(body, outs, *args, flops=0, scalars=0):
    size = sum(a.size for a in args) * 4
    smem = pl.BlockSpec(memory_space=pltpu.SMEM)
    return pl.pallas_call(
        body,
        compiler_params=PARAMS,
        out_shape=outs,
        in_specs=[smem] * scalars + [VMEM] * (len(args) - scalars),
        out_specs=jax.tree.map(lambda _: VMEM, outs),
        cost_estimate=pl.CostEstimate(flops=flops, bytes_accessed=size, transcendentals=0),
    )(*args)


def lane_of(x, c): return jnp.broadcast_to(x[:, c:c+1], (8, LANES))


def row_of(x, r): return jnp.broadcast_to(x[r:r+1, :], (8, LANES))


def base(tiles, lane0):
    row = lax.broadcasted_iota(jnp.int32, (8, LANES), 0)
    n = len(tiles)
    for s in range(n):
        x = tiles[s]
        cols = [lane_of(x, lane0 + 8*s + j) for j in range(8)]
        rest = [[lane_of(tiles[t], lane0 + 8*s + j) for j in range(8)] for t in range(s+1, n)]
        done = None
        for j in range(8):
            rs = lax.rsqrt(row_of(cols[j], j))
            u = row_of(x, j)
            scaled = u * rs
            g = scaled * rs
            done = scaled if done is None else jnp.where(row >= j, scaled, done)
            x = jnp.where(row == j, g, x - cols[j] * g)
            for l in range(j+1, 8):
                cl = row_of(cols[l], j) * (rs * rs)
                cols[l] = jnp.where(row == j, cl, cols[l] - cols[j] * cl)
        tiles[s] = done
        gs = [row_of(x, j) for j in range(8)]
        for i, t in enumerate(range(s+1, n)):
            acc = tiles[t]
            for j in range(8): acc = acc - rest[i][j] * gs[j]
            tiles[t] = acc
    return tiles


def factor_body(core_ref, mine_ref, other_ref, diag_ref, m_ref, u_ref):
    mine, other, first = mine_ref[...], other_ref[...], core_ref[0] == 0
    p = jnp.concatenate(
        [jnp.where(first, mine, other), jnp.where(first, other, mine)], axis=0
    )
    b = BLOCK
    third = p[2 * b :]
    third = jnp.concatenate([third[:, LANES:], third[:, :LANES]], axis=0)
    diag = jnp.concatenate([diag_ref[0:1], diag_ref[1:2]], axis=1)
    blocks = (p[:b], p[b : 2 * b], jnp.concatenate([third, third], axis=1))
    r = lax.broadcasted_iota(jnp.int32, (b, PANEL), 0)
    c = lax.broadcasted_iota(jnp.int32, (b, PANEL), 1)
    for i, rows in enumerate(blocks + (pltpu.roll(p[b : 2 * b], 3 * b, 1),)):
        m_ref[b * i : b * i + b] = rows + jnp.where(r + b * i == c, diag, 0.0)
    lane = lax.broadcasted_iota(jnp.int32, (BLOCK, LANES), 1)
    sub = lax.broadcasted_iota(jnp.int32, (BLOCK, LANES), 0)
    wlane = lax.broadcasted_iota(jnp.int32, (BLOCK, PANEL), 1)
    wsub = lax.broadcasted_iota(jnp.int32, (BLOCK, PANEL), 0)
    for k in range(PANEL // BLOCK):
        odd = k % 2
        seg = m_ref[BLOCK*k:BLOCK*k+BLOCK, LANES*(k//2):LANES*(k//2)+LANES]
        eye = (lane == sub + BLOCK*(1-odd)).astype(jnp.float32)
        own = (lane // BLOCK) == odd
        x = jnp.where(own, seg, eye)
        tiles = base([x[8*t:8*t+8] for t in range(BLOCK//8)], BLOCK*odd)
        x = jnp.concatenate(tiles, axis=0)
        u_ref[BLOCK*k:BLOCK*k+BLOCK, :] = x
        left = jnp.where(own, 0.0, x)
        mrow = m_ref[BLOCK*k:BLOCK*k+BLOCK, :]
        mrow = jnp.where(wlane // BLOCK == k, (wlane == wsub + BLOCK*k).astype(jnp.float32), mrow)
        z = jnp.zeros((BLOCK, PANEL), jnp.float32)
        rhs = jnp.concatenate([mrow, z] if odd else [z, mrow], axis=0)
        nk = lax.dot_general(left, rhs, (((1,),(0,)),((),())), precision=HIGHEST, preferred_element_type=jnp.float32)
        m_ref[BLOCK*k:BLOCK*k+BLOCK, :] = nk
        if k + 1 < PANEL // BLOCK:
            upd = lax.dot_general(nk, nk, (((0,),(0,)),((),())), precision=HIGHEST, preferred_element_type=jnp.float32)
            lo = BLOCK*(k+1)
            below = m_ref[lo:, :]
            wl = lax.broadcasted_iota(jnp.int32, below.shape, 1)
            m_ref[lo:, :] = jnp.where(wl // BLOCK == k, 0.0, below) - upd[lo:, :]


def sum_body(*refs):
    *ins, out = refs
    total = ins[0][...]
    for ref in ins[1:]:
        total = total + ref[...]
    out[...] = total


def copies_body(*refs):
    *ins, out = refs
    total = ins[0][...]
    for ref in ins[1:]:
        total = total + ref[...]
    for i in range(out.shape[0]):
        out[i] = total


def copies(n, *parts):
    return call(copies_body, f32(n, *parts[0].shape), *parts)


def solve_body(inv_ref, panel_ref, o_ref):
    rows = dot(inv_ref[...], panel_ref[...], 1, 0)
    for i in range(o_ref.shape[0]):
        o_ref[i] = rows


def total_body(x_ref, *outs):
    at = 0
    for out in outs:
        rows = slice(at, at + out.shape[0])
        total = x_ref[0, rows]
        for i in range(1, x_ref.shape[0]):
            total = total + x_ref[i, rows]
        out[...] = total
        at += out.shape[0]


def halves(x):
    high = x.astype(jnp.bfloat16)
    return high, (x - high.astype(jnp.float32)).astype(jnp.bfloat16)


def dot_halves(a, b, da, db):
    one = lambda p, q: lax.dot_general(
        p, q, (((da,), (db,)), ((), ())), preferred_element_type=jnp.float32
    )
    return one(a[0], b[0]) + (one(a[0], b[1]) + one(a[1], b[0]))


def turn_body(own_ref, panel_ref, own_high, own_low, panel_high, panel_low):
    own_high[...], own_low[...] = halves(own_ref[0].T)
    panel_high[...], panel_low[...] = halves(panel_ref[...].T)


def terms_body(
    core_ref, own_high, panel_high, panel_low, solved_ref, low_ref, keep_ref, send_ref, low, sem
):
    fetch = pltpu.make_async_copy(low_ref, low, sem)
    fetch.start()
    s = halves(solved_ref[...])
    first = core_ref[0] == 0
    x = dot_halves((panel_high[...], panel_low[...]), s, 1, 0)
    b, w = BLOCK, LANES
    third = jnp.concatenate([x[2 * b + b // 2 : 3 * b, w:], x[2 * b : 2 * b + b // 2, w:]], axis=1)
    lane = lax.broadcasted_iota(jnp.int32, (b, PANEL), 1)
    second = jnp.where(lane < b, pltpu.roll(x[3 * b :], b, 1), x[b : 2 * b])
    x = jnp.concatenate([x[:b], second, third], axis=0)
    piv = x.shape[0] // 2
    at = keep_ref.shape[0] - piv
    keep_ref[at:] = jnp.where(first, x[:piv], x[piv:])
    send_ref[at:] = jnp.where(first, x[piv:], x[:piv])
    one = lambda a, b: jnp.dot(a, b, preferred_element_type=jnp.float32)
    x = one(own_high[...], s[0]) + one(own_high[...], s[1])
    fetch.wait()
    x = x + one(low[...], s[0])
    x = x.reshape(4, 2, at // 4, PANEL)
    keep_ref[:at] = jnp.where(first, x[:, 0], x[:, 1]).reshape(at, PANEL)
    send_ref[:at] = jnp.where(first, x[:, 1], x[:, 0]).reshape(at, PANEL)


def multiply(core, parts, solved, rows):
    high, low, *panels = parts
    return pl.pallas_call(
        terms_body,
        name="terms",
        out_shape=[f32(rows, PANEL)] * 2,
        compiler_params=PARAMS,
        in_specs=[
            pl.BlockSpec(memory_space=pltpu.SMEM), VMEM, VMEM, VMEM, VMEM,
            pl.BlockSpec(memory_space=pltpu.HBM),
        ],
        out_specs=[VMEM] * 2,
        scratch_shapes=[pltpu.VMEM(low.shape, low.dtype), pltpu.SemaphoreType.DMA],
        cost_estimate=pl.CostEstimate(
            flops=9 * high.size * PANEL, bytes_accessed=6 * high.size, transcendentals=0
        ),
    )(core, high, *panels, solved, pltpu.with_memory_space_constraint(low, pltpu.HBM))


def share_body(keep_ref, other_ref, o_ref):
    n = o_ref.shape[0]
    total = keep_ref[...] + other_ref[...]
    rows = (total.shape[0] - PACKED // 2) // n
    for i in range(n):
        o_ref[i, :rows] = total[rows * i : rows * i + rows]
        o_ref[i, rows:] = total[rows * n :]


def finish_body(top_ref, s_ref, m_ref, u_ref, o_ref, left):
    step, per = pl.program_id(0), s_ref.shape[0]
    block = lambda shape, d: lax.broadcasted_iota(jnp.int32, shape, d)

    @pl.when(step == 0)
    def _():
        r, c = block((PANEL, PANEL), 0), block((PANEL, PANEL), 1)
        left[0], left[1] = halves(jnp.where(r >= c, m_ref[...], 0.0))

    o_ref[...] = dot_halves(halves(s_ref[...]), (left[0], left[1]), 1, 1)

    @pl.when((top_ref[0] == 1) & (step < PANEL // per))
    def _():
        r, c = block((PANEL, LANES), 0), block((PANEL, LANES), 1)
        for half in range(PANEL // LANES):
            lanes = slice(LANES * half, LANES * half + LANES)
            inside = (r // BLOCK) == (c + LANES * half) // BLOCK
            upper = jnp.where(inside, u_ref[...], m_ref[:, lanes])
            upper = jnp.where(r <= c + LANES * half, upper, 0.0).T
            for s in range(LANES // per):
                @pl.when(step == half * (LANES // per) + s)
                def _():
                    o_ref[...] = upper[per * s : per * s + per]


def finish(top, rows, m, u):
    width, per = rows.shape[0], 128
    whole = lambda x: pl.BlockSpec(x.shape, lambda i: (0, 0))
    return pl.pallas_call(
        finish_body,
        name="finish",
        compiler_params=PARAMS,
        grid=(width // per,),
        out_shape=f32(width, PANEL),
        in_specs=[
            pl.BlockSpec(memory_space=pltpu.SMEM),
            pl.BlockSpec((per, PANEL), lambda i: (i, 0)),
            whole(m),
            whole(u),
        ],
        out_specs=pl.BlockSpec((per, PANEL), lambda i: (i, 0)),
        scratch_shapes=[pltpu.VMEM((2, PANEL, PANEL), jnp.bfloat16)],
        cost_estimate=pl.CostEstimate(
            flops=2 * width * PANEL * PANEL, bytes_accessed=8 * width * PANEL, transcendentals=0
        ),
    )(top, rows, m, u)


def shards(sizes, coupling, inverse_slabs, barrier_diagonal):
    n_zh, n_x, n_core, n_y, n_zl = (sizes[a] for a in AXES)
    n_xc, n_z = n_x * n_core, n_zh * n_zl
    own = coupling[0]
    depth, width = own.shape
    y, zl = lax.axis_index("y"), lax.axis_index("zl")
    swap = functools.partial(lax.all_to_all, split_axis=0, concat_axis=0)

    one = lambda i: i.astype(jnp.int32).reshape(1)
    per = depth // n_y
    cut = lambda k: own[per * k : per * k + per, :PANEL]
    parts = []
    for k in range(1, n_y):
        parts.append(lax.ppermute(cut(k), ("y", "zl"), [(0, k * n_zl)]))
    first = jnp.where((y == 0) & (zl == 0), cut(0), 0.0)
    mine = call(sum_body, f32(per, PANEL), first, *parts)
    step = n_zl // 2
    while step:
        pairs = [(z, z + step) for z in range(0, n_zl, 2 * step)]
        got = lax.ppermute(mine, "zl", pairs)
        if step > 1:
            mine = mine + got
        step //= 2
    panel = swap(copies(n_y, mine, got), "y").reshape(depth, PANEL)
    inv = swap(copies(n_zl, inverse_slabs[0]), "zl").reshape(per, depth)
    solved = call(solve_body, f32(n_y, per, PANEL), inv, panel, flops=2 * per * depth * PANEL)
    solved = swap(solved, "y").reshape(depth, PANEL)
    core = one(lax.axis_index("core"))
    parts = call(
        turn_body, [bf16(width, depth)] * 2 + [bf16(PANEL, depth)] * 2,
        coupling, panel, flops=10**9,
    )

    n_row, n_piv = width // n_xc, PACKED // 2
    keep, send = multiply(core, parts, solved, n_x * n_row + n_piv)
    other_core = [(0, 1), (1, 0)]
    other = lax.ppermute(send, "core", other_core)
    terms = call(share_body, f32(n_x, n_row + n_piv, PANEL), keep, other)
    terms = swap(terms, "x")
    rows, pivot = call(total_body, [f32(n_row, PANEL), f32(n_piv, PANEL)], terms)

    half = n_zl // 2
    flip = [(z, (z + (half if z // half % 2 else -half)) % n_z) for z in range(n_z)]
    pivot = pivot + lax.ppermute(pivot, ("zh", "zl"), flip)
    other_pivot = lax.ppermute(pivot, "core", other_core)
    other = lax.ppermute(rows, "zh", [(0, 1), (1, 0)])
    rows = swap(copies(n_xc, rows, other), ("x", "core")).reshape(width, PANEL)

    m, u = call(
        factor_body, [f32(PANEL, PANEL), f32(PANEL, LANES)],
        core, pivot, other_pivot, barrier_diagonal.reshape(-1, LANES),
        flops=6 * 10**9, scalars=1,
    )
    top = one((y == 0) & (zl == 0))
    return finish(top, rows, m, u)


def solution(mesh):
    sizes = {"zh": 2, "x": 4, "core": 2, "y": 4, "zl": 8}
    fine = Mesh(mesh.devices.reshape([sizes[a] for a in AXES]), AXES)
    return jax.shard_map(
        functools.partial(shards, sizes),
        mesh=fine,
        in_specs=(
            P(("zh", "x", "core"), None, ("y", "zl")),
            P(("zh", "x", "core"), ("y", "zl"), None),
            P(),
        ),
        out_specs=P(("y", "zl"), None),
        check_vma=False,
    )
```

```python
import functools

import jax
import jax.numpy as jnp
from jax import lax
from jax.experimental import pallas as pl
from jax.experimental.pallas import tpu as pltpu
from jax.sharding import Mesh, PartitionSpec as P

PANEL = 256
BLOCK = 64
LANES = 128
PACKED = 160
AXES = ("zh", "x", "core", "y", "zl")
HIGHEST = lax.Precision.HIGHEST
VMEM = pl.BlockSpec(memory_space=pltpu.VMEM)
PARAMS = pltpu.CompilerParams(vmem_limit_bytes=12 << 20)


def f32(*shape):
    return jax.ShapeDtypeStruct(shape, jnp.float32)


def bf16(*shape):
    return jax.ShapeDtypeStruct(shape, jnp.bfloat16)


def dot(a, b, da, db):
    return lax.dot_general(
        a, b, (((da,), (db,)), ((), ())), precision=HIGHEST, preferred_element_type=jnp.float32
    )


def call(body, outs, *args, flops=0, scalars=0):
    size = sum(a.size for a in args) * 4
    smem = pl.BlockSpec(memory_space=pltpu.SMEM)
    return pl.pallas_call(
        body,
        compiler_params=PARAMS,
        out_shape=outs,
        in_specs=[smem] * scalars + [VMEM] * (len(args) - scalars),
        out_specs=jax.tree.map(lambda _: VMEM, outs),
        cost_estimate=pl.CostEstimate(flops=flops, bytes_accessed=size, transcendentals=0),
    )(*args)


def lane_of(x, c): return jnp.broadcast_to(x[:, c:c+1], (8, LANES))


def row_of(x, r): return jnp.broadcast_to(x[r:r+1, :], (8, LANES))


def base(tiles, lane0):
    row = lax.broadcasted_iota(jnp.int32, (8, LANES), 0)
    n = len(tiles)
    columns = lambda t, group: [lane_of(tiles[t], lane0 + 8 * group + j) for j in range(8)]
    tree = lambda p: ((p[0] + p[1]) + (p[2] + p[3])) + ((p[4] + p[5]) + (p[6] + p[7]))
    cols = columns(0, 0)
    for s in range(n):
        x = tiles[s]
        last = s + 1 == n
        after = [] if last else columns(s, s + 1)
        ahead = [] if last else columns(s + 1, s + 1)
        rest = [columns(t, s) for t in range(s + 1, n)]
        done = None
        for j in range(8):
            rs = lax.rsqrt(row_of(cols[j], j))
            r2 = rs * rs
            col = cols[j]

            def eliminate(v):
                pivot_row = row_of(v, j)
                return jnp.where(row == j, pivot_row * r2, v - (col * pivot_row) * r2)

            scaled = row_of(x, j) * rs
            done = scaled if done is None else jnp.where(row >= j, scaled, done)
            cols = cols[: j + 1] + [eliminate(v) for v in cols[j + 1 :]]
            after = [eliminate(v) for v in after]
            x = eliminate(x)
        tiles[s] = done
        if not last:
            cols = [
                ahead[m] - tree([rest[0][j] * row_of(after[m], j) for j in range(8)])
                for m in range(8)
            ]
        rows = [row_of(x, j) for j in range(8)]
        for i, t in enumerate(range(s + 1, n)):
            tiles[t] = tiles[t] - tree([rest[i][j] * rows[j] for j in range(8)])
    return tiles


def factor_body(core_ref, mine_ref, other_ref, diag_ref, m_ref, u_ref):
    mine, other, first = mine_ref[...], other_ref[...], core_ref[0] == 0
    p = jnp.concatenate(
        [jnp.where(first, mine, other), jnp.where(first, other, mine)], axis=0
    )
    b = BLOCK
    third = p[2 * b :]
    third = jnp.concatenate([third[:, LANES:], third[:, :LANES]], axis=0)
    diag = jnp.concatenate([diag_ref[0:1], diag_ref[1:2]], axis=1)
    blocks = (p[:b], p[b : 2 * b], jnp.concatenate([third, third], axis=1))
    r = lax.broadcasted_iota(jnp.int32, (b, PANEL), 0)
    c = lax.broadcasted_iota(jnp.int32, (b, PANEL), 1)
    for i, rows in enumerate(blocks + (pltpu.roll(p[b : 2 * b], 3 * b, 1),)):
        m_ref[b * i : b * i + b] = rows + jnp.where(r + b * i == c, diag, 0.0)
    lane = lax.broadcasted_iota(jnp.int32, (BLOCK, LANES), 1)
    sub = lax.broadcasted_iota(jnp.int32, (BLOCK, LANES), 0)
    wlane = lax.broadcasted_iota(jnp.int32, (BLOCK, PANEL), 1)
    wsub = lax.broadcasted_iota(jnp.int32, (BLOCK, PANEL), 0)
    for k in range(PANEL // BLOCK):
        odd = k % 2
        seg = m_ref[BLOCK*k:BLOCK*k+BLOCK, LANES*(k//2):LANES*(k//2)+LANES]
        eye = (lane == sub + BLOCK*(1-odd)).astype(jnp.float32)
        own = (lane // BLOCK) == odd
        x = jnp.where(own, seg, eye)
        tiles = base([x[8*t:8*t+8] for t in range(BLOCK//8)], BLOCK*odd)
        x = jnp.concatenate(tiles, axis=0)
        u_ref[BLOCK*k:BLOCK*k+BLOCK, :] = x
        left = jnp.where(own, 0.0, x)
        mrow = m_ref[BLOCK*k:BLOCK*k+BLOCK, :]
        mrow = jnp.where(wlane // BLOCK == k, (wlane == wsub + BLOCK*k).astype(jnp.float32), mrow)
        z = jnp.zeros((BLOCK, PANEL), jnp.float32)
        rhs = jnp.concatenate([mrow, z] if odd else [z, mrow], axis=0)
        nk = dot_halves(halves(left), halves(rhs), 1, 0)
        m_ref[BLOCK*k:BLOCK*k+BLOCK, :] = nk
        if k + 1 < PANEL // BLOCK:
            high, low = halves(nk)
            upd = dot_halves((high.T, low.T), (high, low), 1, 0)
            lo = BLOCK*(k+1)
            below = m_ref[lo:, :]
            wl = lax.broadcasted_iota(jnp.int32, below.shape, 1)
            m_ref[lo:, :] = jnp.where(wl // BLOCK == k, 0.0, below) - upd[lo:, :]


def sum_body(*refs):
    *ins, out = refs
    total = ins[0][...]
    for ref in ins[1:]:
        total = total + ref[...]
    out[...] = total


def copies_body(*refs):
    *ins, out = refs
    total = ins[0][...]
    for ref in ins[1:]:
        total = total + ref[...]
    for i in range(out.shape[0]):
        out[i] = total


def copies(n, *parts):
    return call(copies_body, f32(n, *parts[0].shape), *parts)


def solve_body(inv_ref, panel_ref, o_ref):
    rows = dot(inv_ref[...], panel_ref[...], 1, 0)
    for i in range(o_ref.shape[0]):
        o_ref[i] = rows


def total_body(x_ref, *outs):
    at = 0
    for out in outs:
        rows = slice(at, at + out.shape[0])
        total = x_ref[0, rows]
        for i in range(1, x_ref.shape[0]):
            total = total + x_ref[i, rows]
        out[...] = total
        at += out.shape[0]


def halves(x):
    high = x.astype(jnp.bfloat16)
    return high, (x - high.astype(jnp.float32)).astype(jnp.bfloat16)


def dot_halves(a, b, da, db):
    one = lambda p, q: lax.dot_general(
        p, q, (((da,), (db,)), ((), ())), preferred_element_type=jnp.float32
    )
    return one(a[0], b[0]) + (one(a[0], b[1]) + one(a[1], b[0]))


def turn_body(own_ref, panel_ref, own_high, own_low, panel_high, panel_low):
    own_high[...], own_low[...] = halves(own_ref[0].T)
    panel_high[...], panel_low[...] = halves(panel_ref[...].T)


def terms_body(
    core_ref, own_high, panel_high, panel_low, solved_ref, low_ref, keep_ref, send_ref, low, sem
):
    fetch = pltpu.make_async_copy(low_ref, low, sem)
    fetch.start()
    s = halves(solved_ref[...])
    first = core_ref[0] == 0
    x = dot_halves((panel_high[...], panel_low[...]), s, 1, 0)
    b, w = BLOCK, LANES
    third = jnp.concatenate([x[2 * b + b // 2 : 3 * b, w:], x[2 * b : 2 * b + b // 2, w:]], axis=1)
    lane = lax.broadcasted_iota(jnp.int32, (b, PANEL), 1)
    second = jnp.where(lane < b, pltpu.roll(x[3 * b :], b, 1), x[b : 2 * b])
    x = jnp.concatenate([x[:b], second, third], axis=0)
    piv = x.shape[0] // 2
    at = keep_ref.shape[0] - piv
    keep_ref[at:] = jnp.where(first, x[:piv], x[piv:])
    send_ref[at:] = jnp.where(first, x[piv:], x[:piv])
    one = lambda a, b: jnp.dot(a, b, preferred_element_type=jnp.float32)
    x = one(own_high[...], s[0]) + one(own_high[...], s[1])
    fetch.wait()
    x = x + one(low[...], s[0])
    x = x.reshape(4, 2, at // 4, PANEL)
    keep_ref[:at] = jnp.where(first, x[:, 0], x[:, 1]).reshape(at, PANEL)
    send_ref[:at] = jnp.where(first, x[:, 1], x[:, 0]).reshape(at, PANEL)


def multiply(core, parts, solved, rows):
    high, low, *panels = parts
    return pl.pallas_call(
        terms_body,
        name="terms",
        out_shape=[f32(rows, PANEL)] * 2,
        compiler_params=PARAMS,
        in_specs=[
            pl.BlockSpec(memory_space=pltpu.SMEM), VMEM, VMEM, VMEM, VMEM,
            pl.BlockSpec(memory_space=pltpu.HBM),
        ],
        out_specs=[VMEM] * 2,
        scratch_shapes=[pltpu.VMEM(low.shape, low.dtype), pltpu.SemaphoreType.DMA],
        cost_estimate=pl.CostEstimate(
            flops=9 * high.size * PANEL, bytes_accessed=6 * high.size, transcendentals=0
        ),
    )(core, high, *panels, solved, pltpu.with_memory_space_constraint(low, pltpu.HBM))


def share_body(keep_ref, other_ref, o_ref):
    n = o_ref.shape[0]
    total = keep_ref[...] + other_ref[...]
    rows = (total.shape[0] - PACKED // 2) // n
    for i in range(n):
        o_ref[i, :rows] = total[rows * i : rows * i + rows]
        o_ref[i, rows:] = total[rows * n :]


def finish_body(top_ref, s_ref, m_ref, u_ref, o_ref, left):
    step, per = pl.program_id(0), s_ref.shape[0]
    block = lambda shape, d: lax.broadcasted_iota(jnp.int32, shape, d)

    @pl.when(step == 0)
    def _():
        r, c = block((PANEL, PANEL), 0), block((PANEL, PANEL), 1)
        left[0], left[1] = halves(jnp.where(r >= c, m_ref[...], 0.0))

    o_ref[...] = dot_halves(halves(s_ref[...]), (left[0], left[1]), 1, 1)

    @pl.when((top_ref[0] == 1) & (step * per < PANEL))
    def _():
        r, c = block((PANEL, LANES), 0), block((PANEL, LANES), 1)
        for half in range(PANEL // LANES):
            lanes = slice(LANES * half, LANES * half + LANES)
            inside = (r // BLOCK) == (c + LANES * half) // BLOCK
            upper = jnp.where(inside, u_ref[...], m_ref[:, lanes])
            o_ref[lanes] = jnp.where(r <= c + LANES * half, upper, 0.0).T


def finish(top, rows, m, u):
    width, per = rows.shape[0], 256
    whole = lambda x: pl.BlockSpec(x.shape, lambda i: (0, 0))
    return pl.pallas_call(
        finish_body,
        name="finish",
        compiler_params=PARAMS,
        grid=(width // per,),
        out_shape=f32(width, PANEL),
        in_specs=[
            pl.BlockSpec(memory_space=pltpu.SMEM),
            pl.BlockSpec((per, PANEL), lambda i: (i, 0)),
            whole(m),
            whole(u),
        ],
        out_specs=pl.BlockSpec((per, PANEL), lambda i: (i, 0)),
        scratch_shapes=[pltpu.VMEM((2, PANEL, PANEL), jnp.bfloat16)],
        cost_estimate=pl.CostEstimate(
            flops=2 * width * PANEL * PANEL, bytes_accessed=8 * width * PANEL, transcendentals=0
        ),
    )(top, rows, m, u)


def shards(sizes, coupling, inverse_slabs, barrier_diagonal):
    n_zh, n_x, n_core, n_y, n_zl = (sizes[a] for a in AXES)
    n_xc, n_z = n_x * n_core, n_zh * n_zl
    own = coupling[0]
    depth, width = own.shape
    y, zl = lax.axis_index("y"), lax.axis_index("zl")
    swap = functools.partial(lax.all_to_all, split_axis=0, concat_axis=0)

    one = lambda i: i.astype(jnp.int32).reshape(1)
    per = depth // n_y
    cut = lambda k: own[per * k : per * k + per, :PANEL]
    parts = []
    for k in range(1, n_y):
        parts.append(lax.ppermute(cut(k), ("y", "zl"), [(0, k * n_zl)]))
    first = jnp.where((y == 0) & (zl == 0), cut(0), 0.0)
    mine = call(sum_body, f32(per, PANEL), first, *parts)
    step = n_zl // 2
    while step:
        pairs = [(z, z + step) for z in range(0, n_zl, 2 * step)]
        got = lax.ppermute(mine, "zl", pairs)
        if step > 1:
            mine = mine + got
        step //= 2
    panel = swap(copies(n_y, mine, got), "y").reshape(depth, PANEL)
    inv = swap(copies(n_zl, inverse_slabs[0]), "zl").reshape(per, depth)
    solved = call(solve_body, f32(n_y, per, PANEL), inv, panel, flops=2 * per * depth * PANEL)
    solved = swap(solved, "y").reshape(depth, PANEL)
    core = one(lax.axis_index("core"))
    parts = call(
        turn_body, [bf16(width, depth)] * 2 + [bf16(PANEL, depth)] * 2,
        coupling, panel, flops=10**9,
    )

    n_row, n_piv = width // n_xc, PACKED // 2
    keep, send = multiply(core, parts, solved, n_x * n_row + n_piv)
    other_core = [(0, 1), (1, 0)]
    other = lax.ppermute(send, "core", other_core)
    terms = call(share_body, f32(n_x, n_row + n_piv, PANEL), keep, other)
    terms = swap(terms, "x")
    rows, pivot = call(total_body, [f32(n_row, PANEL), f32(n_piv, PANEL)], terms)

    half = n_zl // 2
    flip = [(z, (z + (half if z // half % 2 else -half)) % n_z) for z in range(n_z)]
    pivot = pivot + lax.ppermute(pivot, ("zh", "zl"), flip)
    other_pivot = lax.ppermute(pivot, "core", other_core)
    other = lax.ppermute(rows, "zh", [(0, 1), (1, 0)])
    rows = swap(copies(n_xc, rows, other), ("x", "core")).reshape(width, PANEL)

    m, u = call(
        factor_body, [f32(PANEL, PANEL), f32(PANEL, LANES)],
        core, pivot, other_pivot, barrier_diagonal.reshape(-1, LANES),
        flops=6 * 10**9, scalars=1,
    )
    top = one((y == 0) & (zl == 0))
    return finish(top, rows, m, u)


def solution(mesh):
    sizes = {"zh": 2, "x": 4, "core": 2, "y": 4, "zl": 8}
    fine = Mesh(mesh.devices.reshape([sizes[a] for a in AXES]), AXES)
    return jax.shard_map(
        functools.partial(shards, sizes),
        mesh=fine,
        in_specs=(
            P(("zh", "x", "core"), None, ("y", "zl")),
            P(("zh", "x", "core"), ("y", "zl"), None),
            P(),
        ),
        out_specs=P(("y", "zl"), None),
        check_vma=False,
    )
```
